128 devices in a mesh: rg: 4 (over y_hi, core), az: 32 (over y_lo, x, z).
Axes of the slice: x: 4, y: 4 (y_hi: 2, y_lo: 2; y = y_hi * 2 + y_lo), z: 4, core: 2. Of those that a mesh axis runs over, the one named last changes fastest.
Arguments:
- raw_pulses: bfloat16 [2, 2048, 65536], P(None, ('rg', 'az')), may hold values from -6 to 6
- range_phase: float32 [65536], replicated, may hold values from -3.140625 to 3.140625
- azimuth_rate: float32 [65536], P(('rg', 'az')), may hold values from 40 to 400
- conc_azimuth: float32 [2048], replicated, may hold values from 0.2 to 1
- conc_range: float32 [65536], replicated, may hold values from 0.2 to 1
Outputs:
- edge_azimuth: float32 [2048, 65536], P(None, ('rg', 'az'))
- edge_range: float32 [2048, 65536], P(('rg', 'az'))
The draws below stay inside these ranges and needn't reach their ends.
All inputs are finite; a program needn't handle non-finite values.
Results may differ from the reference program's by a relative error of at most 0.028.
Values may be sent and summed in bfloat16 or wider, within the bound.
No kernel may reach another device: no remote copies, remote signals or barrier semaphores. Data moves between devices by JAX's collectives and lax.ppermute only.
A program may use at most 128 MiB of HBM per device.

```python
import math
import jax
import jax.numpy as jnp
from jax import lax

RA = 256
RB = 256
QA = 32
QB = 64
BINS = 65536
PULSES = 2048


def level_of(key, dims, split, least, top_value):
    def one(axis_at, blocks):
        draws = jax.random.uniform(jax.random.fold_in(jax.random.fold_in(key, 6), axis_at), (blocks,), jnp.float32, least / len(split), top_value / len(split))
        return jnp.repeat(jnp.exp(draws), dims[axis_at] // blocks).reshape((-1,) + (1,) * (len(dims) - axis_at - 1))

    gain = one(*split[0])
    for cut in split[1:]:
        gain = gain * one(*cut)
    return gain


def bell_draw(rng, dims, spread, bound, shards=(), held_as=jnp.bfloat16):
    array = spread * jax.random.normal(rng, dims, jnp.float32)
    if shards:
        array = array * level_of(rng, dims, shards, -0.22, 0.18)
    return jnp.clip(array, -bound, bound).astype(held_as)


def setup_inputs(seed: int = 0) -> dict:
    streams_of = jax.random.split(jax.random.key(seed), 6)
    return {
        "raw_pulses": bell_draw(streams_of[0], (2, PULSES, BINS), 1.0, 6.0, ((1, 128),)),
        "range_phase": jnp.clip(jax.random.uniform(streams_of[1], (BINS,), jnp.float32, -3.140625, 3.140625), -3.140625, 3.140625),
        "azimuth_rate": jnp.clip(jnp.exp(math.log(400.0) - 2.3025851 * jax.random.uniform(streams_of[2], (BINS,), jnp.float32) ** level_of(streams_of[2], (BINS,), ((0, 128),), -0.2, 0.2)), 40.0, 400.0),
        "conc_azimuth": jnp.clip(jax.random.uniform(streams_of[3], (PULSES,), jnp.float32, 0.2, 1.0), 0.2, 1.0),
        "conc_range": jnp.clip(jax.random.uniform(streams_of[4], (BINS,), jnp.float32, 0.2, 1.0), 0.2, 1.0),
    }


def dft_table(length, sign):
    indices = jnp.arange(length, dtype=jnp.int32)
    product = indices[:, None] * indices[None, :] % length
    angles = sign * 2.0 * math.pi / length * product.astype(jnp.float32)
    factor = 1.0 / math.sqrt(length)
    return ((jnp.cos(angles) * factor).astype(jnp.bfloat16), (jnp.sin(angles) * factor).astype(jnp.bfloat16))

def twiddle(first_len, second, sign):
    length_all = first_len * second
    product = jnp.arange(first_len, dtype=jnp.int32)[:, None] * jnp.arange(second, dtype=jnp.int32)[None, :] % length_all
    angles = sign * 2.0 * math.pi / length_all * product.astype(jnp.float32)
    return (jnp.cos(angles), jnp.sin(angles))

def signed_freq(first_len, second):
    length_all = first_len * second
    freqs = jnp.arange(first_len, dtype=jnp.int32)[:, None] + first_len * jnp.arange(second, dtype=jnp.int32)[None, :]
    return jnp.where(freqs < length_all // 2, freqs, freqs - length_all)

def contract(form, matrix, pieces):
    mat_real = matrix[0].astype(jnp.float32)
    mat_imag = matrix[1].astype(jnp.float32)
    if len(pieces) == 1:
        single = pieces[0].astype(jnp.float32)
        return (jnp.einsum(form, mat_real, single), jnp.einsum(form, mat_imag, single))
    real_part = pieces[0].astype(jnp.float32)
    imag_part = pieces[1].astype(jnp.float32)
    return (jnp.einsum(form, mat_real, real_part) - jnp.einsum(form, mat_imag, imag_part), jnp.einsum(form, mat_real, imag_part) + jnp.einsum(form, mat_imag, real_part))

def rotate(pieces, cosine, sine_part):
    return (pieces[0] * cosine - pieces[1] * sine_part, pieces[0] * sine_part + pieces[1] * cosine)

def to_half(pieces):
    return tuple((piece.astype(jnp.bfloat16) for piece in pieces))

def forward(pieces, first_len, second, forms, expand):
    sectioned = contract(forms[0], dft_table(first_len, -1.0), pieces)
    cosine, sine_part = twiddle(first_len, second, -1.0)
    sectioned = to_half(rotate(sectioned, expand(cosine), expand(sine_part)))
    return contract(forms[1], dft_table(second, -1.0), sectioned)

def inverse(pieces, first_len, second, forms, expand, real_only):
    sectioned = contract(forms[2], dft_table(second, 1.0), pieces)
    cosine, sine_part = twiddle(first_len, second, 1.0)
    sectioned = to_half(rotate(sectioned, expand(cosine), expand(sine_part)))
    if real_only:
        mat_real, mat_imag = dft_table(first_len, 1.0)
        return jnp.einsum(forms[3], mat_real.astype(jnp.float32), sectioned[0].astype(jnp.float32)) - jnp.einsum(forms[3], mat_imag.astype(jnp.float32), sectioned[1].astype(jnp.float32))
    return contract(forms[3], dft_table(first_len, 1.0), sectioned)

def range_forms():
    return ('kn,pnb->pkb', 'bm,pkb->pkm', 'mb,pkm->pkb', 'nk,pkb->pnb')

def azimuth_forms():
    return ('ka,abr->kbr', 'bm,kbr->kmr', 'mb,kmr->kbr', 'nk,kbr->nbr')

def range_expand(table):
    return table[None]

def azimuth_expand(table):
    return table[:, :, None]

def concentrate(values, first_len, second, factors, forms, expand):
    spectrum = forward((values,), first_len, second, forms, expand)
    signs = jnp.sign(signed_freq(first_len, second)).astype(jnp.float32)
    weights = expand(signs * factors.reshape(second, first_len).T)
    jumped = to_half((-weights * spectrum[1], weights * spectrum[0]))
    return inverse(jumped, first_len, second, forms, expand, True)

def range_compress(pieces, range_phase):
    count = pieces[0].shape[0]
    shaped = tuple((piece.reshape(count, RA, RB) for piece in pieces))
    spectrum = forward(shaped, RA, RB, range_forms(), range_expand)
    grid = range_phase.reshape(RB, RA).T
    spectrum = to_half(rotate(spectrum, jnp.cos(grid)[None], jnp.sin(grid)[None]))
    result = inverse(spectrum, RA, RB, range_forms(), range_expand, False)
    return tuple((piece.astype(jnp.bfloat16).reshape(count, RA * RB) for piece in result))

def azimuth_part(pieces, rates, conc_azimuth):
    width = pieces[0].shape[1]
    shaped = tuple((piece.reshape(QA, QB, width) for piece in pieces))
    spectrum = forward(shaped, QA, QB, azimuth_forms(), azimuth_expand)
    signed = signed_freq(QA, QB).astype(jnp.float32) / (QA * QB)
    phases = rates[None, None, :] * (signed * signed)[:, :, None]
    spectrum = to_half(rotate(spectrum, jnp.cos(phases), jnp.sin(phases)))
    picture = inverse(spectrum, QA, QB, azimuth_forms(), azimuth_expand, False)
    magnitude = jnp.sqrt(picture[0] * picture[0] + picture[1] * picture[1]).astype(jnp.bfloat16)
    edges = concentrate(magnitude, QA, QB, conc_azimuth, azimuth_forms(), azimuth_expand)
    return (edges.reshape(QA * QB, width), magnitude.reshape(QA * QB, width))

def range_concentrate(rows, conc_range):
    count = rows.shape[0]
    edges = concentrate(rows.reshape(count, RA, RB), RA, RB, conc_range, range_forms(), range_expand)
    return edges.reshape(count, RA * RB)

def reference(raw_pulses, range_phase, azimuth_rate, conc_azimuth, conc_range):
    block_size = 64
    block_count = PULSES // block_size
    blocks = raw_pulses.reshape(2, block_count, block_size, BINS).transpose(1, 0, 2, 3)

    def per_block(block):
        return jnp.stack(range_compress((block[0], block[1]), range_phase))
    compressed = lax.map(per_block, blocks).transpose(1, 0, 2, 3).reshape(2, PULSES, BINS)
    bin_block = min(512, BINS)
    bin_count = BINS // bin_block
    columns = compressed.reshape(2, PULSES, bin_count, bin_block).transpose(2, 0, 1, 3)
    rate_blocks = azimuth_rate.reshape(bin_count, bin_block)

    def per_column(operands):
        column, rates = operands
        return azimuth_part((column[0], column[1]), rates, conc_azimuth)
    edges, magnitudes = lax.map(per_column, (columns, rate_blocks))
    edge_azimuth = edges.transpose(1, 0, 2).reshape(PULSES, BINS)
    magnitude = magnitudes.transpose(1, 0, 2).reshape(PULSES, BINS)
    row_blocks = magnitude.reshape(block_count, block_size, BINS)

    def per_rows(rows):
        return range_concentrate(rows, conc_range)
    edge_range = lax.map(per_rows, row_blocks).reshape(PULSES, BINS)
    return (edge_azimuth, edge_range)
```

```python
import math

import jax
import jax.numpy as jnp
import numpy as np
from jax import lax
from jax.experimental import pallas as pl
from jax.experimental.pallas import tpu as pltpu
from jax.sharding import PartitionSpec as P

AXES = ("rg", "az")
BINS = 65536
PULSES = 2048
ROWS = 16
OWNERS = 128
WIDTH = 512
LOW = jnp.bfloat16
F32 = jnp.float32


def roots(exponents, length):
    angles = 2.0 * math.pi / length * (exponents % length)
    return np.cos(angles) + 1j * np.sin(angles)


def left_form(matrix):
    return np.block([[matrix.real, -matrix.imag], [matrix.imag, matrix.real]])


def right_form(matrix):
    return np.block([[matrix.real, matrix.imag], [-matrix.imag, matrix.real]])


def low(table):
    return np.asarray(table, np.float32).astype(LOW)


def range_tables():
    k = np.arange(128)[:, None]
    j = np.arange(128)[None, :]
    even = roots(2 * j * k, 256) / 16.0
    odd = roots((2 * j + 1) * k, 256) / 16.0
    first = np.stack([left_form(even.conj()), left_form(odd.conj())])
    second = np.stack([right_form(even.conj()), right_form(odd.conj())])
    third = np.stack([right_form(even.T), right_form(odd.T)])
    fourth = np.stack([left_form(even.T), left_form(odd.T)])
    return tuple(low(t) for t in (first, second, third, fourth))


def range_turns(rows):
    table = roots(np.arange(rows)[:, None] * np.arange(256)[None, :], BINS)
    return np.stack([table.real, table.imag]).astype(np.float32)


def real_range_tables():
    k = np.arange(128)[:, None]
    n = np.concatenate([2 * np.arange(128), 2 * np.arange(128) + 1])[None, :]
    base = roots(k * n, 256) / 16.0
    mirror = np.cos(math.pi * n) / 16.0
    first = np.concatenate([base.real, mirror, -base.imag[1:]], 0)
    last = np.concatenate([base.real.T, mirror.T, -base.imag[1:].T], 1)
    return low(first), low(last)


def azimuth_tables():
    s = np.arange(128)
    outer = roots(-s[:, None] * s[None, :], 128) / math.sqrt(128.0)
    full = left_form(outer).reshape(2, 16, 8, 256).transpose(1, 0, 2, 3).reshape(256, 256)
    group = np.arange(16)[:, None, None, None]
    eight = np.arange(8)[None, None, None, :]
    fb = np.arange(16)[None, :, None, None]
    p = np.arange(16)[None, None, :, None]
    inner = roots(-p * (8 * group + eight + 128 * fb), PULSES) / 4.0
    pair = np.stack([np.stack([inner.real, -inner.imag], 3), np.stack([inner.imag, inner.real], 3)], 2)
    forward = pair.reshape(16, 32, 256)
    backward = pair.transpose(0, 3, 4, 1, 2, 5).reshape(16, 32, 256)
    return low(full), low(full.T), low(forward), low(backward)


def dot(a, b):
    return jnp.dot(a, b, preferred_element_type=F32)


def beside(a, b):
    return jnp.concatenate([a, b], 1)


def above(a, b):
    return jnp.concatenate([a, b], 0)


def forward_spectrum(parts, turns, second):
    sums, gaps = [], []
    for re, im, rows in parts:
        c, s = turns[0, rows, :], turns[1, rows, :]
        tr = re * c + im * s
        ti = im * c - re * s
        sums.append(beside(tr[:, :128] + tr[:, 128:], ti[:, :128] + ti[:, 128:]).astype(LOW))
        gaps.append(beside(tr[:, :128] - tr[:, 128:], ti[:, :128] - ti[:, 128:]).astype(LOW))
    return (
        dot(jnp.concatenate(sums, 0), second[0]),
        dot(jnp.concatenate(gaps, 0), second[1]),
    )


def back_section(even, odd, turns, third):
    even = dot(even, third[0])
    odd = dot(odd, third[1])
    rows = even.shape[0]
    halves = []
    for h, b in enumerate((even + odd, even - odd)):
        c = turns[0, :rows, h * 128 : h * 128 + 128]
        s = turns[1, :rows, h * 128 : h * 128 + 128]
        re, im = b[:, :128], b[:, 128:]
        halves.append((re * c - im * s, re * s + im * c))
    return halves


def compress_kernel(raw, phase, first, second, third, fourth, turns, out, xs, os):
    def spread(n, _):
        for u in range(4):
            at = n * 4 + u
            for c in range(2):
                v = raw[c, :, pl.ds(pl.multiple_of(at * 256, 256), 256)].astype(F32)
                row = pl.multiple_of(at * ROWS, ROWS)
                xs[c, 0, pl.ds(row, ROWS), :] = v[:, :128]
                xs[c, 1, pl.ds(row, ROWS), :] = v[:, 128:]
        return 0

    lax.fori_loop(0, 64, spread, 0)

    def one(p):
        def load(odd):
            def half(c):
                at = pl.ds(odd * ROWS + p, 128, stride=2 * ROWS)
                return beside(xs[c, 0, at, :], xs[c, 1, at, :])

            return above(half(0), half(1)).astype(LOW)

        even = dot(first[0], load(0))
        odd = dot(first[1], load(1))
        lo, hi = even + odd, even - odd
        parts = [(v[:128], v[128:], slice(r, r + 128)) for v, r in ((lo, 0), (hi, 128))]
        turned = []
        for e, z in enumerate(forward_spectrum(parts, turns, second)):
            c = phase[0, :, e * 128 : e * 128 + 128]
            s = phase[1, :, e * 128 : e * 128 + 128]
            re, im = z[:, :128], z[:, 128:]
            turned.append(beside(re * c - im * s, re * s + im * c).astype(LOW))
        (r0, i0), (r1, i1) = back_section(turned[0], turned[1], turns, third)
        re, im = beside(r0, r1), beside(i0, i1)
        sums = above(re[:128] + re[128:], im[:128] + im[128:]).astype(LOW)
        gaps = above(re[:128] - re[128:], im[:128] - im[128:]).astype(LOW)
        for o, c in enumerate((dot(fourth[0], sums), dot(fourth[1], gaps))):
            for part in range(2):
                for h in range(2):
                    os[part * 4 + o * 2 + h, pl.ds(p, 128, stride=ROWS), :] = c[
                        part * 128 : part * 128 + 128, h * 128 : h * 128 + 128
                    ]

    def pair(i, _):
        one(2 * i)
        one(2 * i + 1)
        return 0

    lax.fori_loop(0, ROWS // 2, pair, 0)

    def gather(n, _):
        rows = pl.ds(pl.multiple_of(n * 128, 128), 128)
        for k in range(8):
            v = os[k, rows, :].astype(LOW).reshape(8, ROWS, 128)
            out[pl.ds(n * 8, 8), :, k * 128 : k * 128 + 128] = v
        return 0

    lax.fori_loop(0, 16, gather, 0)


def range_compress(raw, phase, tables, turns):
    return pl.pallas_call(
        compress_kernel,
        out_shape=jax.ShapeDtypeStruct((OWNERS, ROWS, 1024), LOW),
        scratch_shapes=[
            pltpu.VMEM((2, 2, 256 * ROWS, 128), F32),
            pltpu.VMEM((8, OWNERS * ROWS, 128), F32),
        ],
        name="range_compress",
    )(raw, phase, *tables, turns)


def spread_rows(source, xs):
    def move(n, _):
        rows = pl.ds(pl.multiple_of(n * 128, 128), 128)
        for h in range(2):
            v = source[pl.ds(n * 8, 8), :, h * 128 : h * 128 + 128].astype(F32)
            xs[h, rows, :] = v.reshape(128, 128)
        return 0

    lax.fori_loop(0, 16, move, 0)


def pulse_rows(xs, p):
    at = pl.ds(p, 128, stride=ROWS)
    return beside(xs[0, at, :], xs[1, at, :])


def picture_kernel(re, im, phase, full, back, forward, backward, out, xr, xi, ys, vs, ms):
    spread_rows(re, xr)
    spread_rows(im, xi)

    def outer(p, _):
        x = above(pulse_rows(xr, p), pulse_rows(xi, p)).astype(LOW)
        ys[p] = dot(full[...], x).astype(LOW)
        return 0

    lax.fori_loop(0, 16, outer, 0, unroll=4)

    def inner(g, _):
        rows = pl.ds(pl.multiple_of(g * 16, 16), 16)
        y = dot(forward[g], ys[:, rows, :].reshape(256, 256)).reshape(16, 2, 8, 256)
        c = phase[0, g].reshape(16, 8, 256)
        s = phase[1, g].reshape(16, 8, 256)
        zr = y[:, 0] * c - y[:, 1] * s
        zi = y[:, 0] * s + y[:, 1] * c
        z = jnp.stack([zr, zi], 1).reshape(256, 256).astype(LOW)
        vs[:, rows, :] = dot(backward[g], z).astype(LOW).reshape(16, 16, 256)
        return 0

    lax.fori_loop(0, 16, inner, 0, unroll=2)

    def last(p, _):
        x = dot(back[...], vs[p])
        a, b = x[:128], x[128:]
        m = jnp.sqrt(a * a + b * b)
        at = pl.ds(p, 128, stride=ROWS)
        ms[0, at, :] = m[:, :128]
        ms[1, at, :] = m[:, 128:]
        return 0

    lax.fori_loop(0, 16, last, 0, unroll=4)

    def gather(n, _):
        rows = pl.ds(pl.multiple_of(n * 128, 128), 128)
        for h in range(2):
            v = ms[h, rows, :].astype(LOW).reshape(8, ROWS, 128)
            out[pl.ds(n * 8, 8), :, h * 128 : h * 128 + 128] = v
        return 0

    lax.fori_loop(0, 16, gather, 0)


def whole(shape):
    return pl.BlockSpec(shape, lambda i: (0,) * len(shape))


def azimuth_picture(received, phase, full, back, forward, backward):
    return pl.pallas_call(
        picture_kernel,
        grid=(2,),
        in_specs=[
            pl.BlockSpec((OWNERS, ROWS, 256), lambda i: (0, 0, i)),
            pl.BlockSpec((OWNERS, ROWS, 256), lambda i: (0, 0, i + 2)),
            pl.BlockSpec((2, 16, 128, 256), lambda i: (0, 0, 0, i)),
            whole((256, 256)),
            whole((256, 256)),
            whole((16, 256, 256)),
            whole((16, 256, 256)),
        ],
        out_specs=pl.BlockSpec((OWNERS, ROWS, 256), lambda i: (0, 0, i)),
        out_shape=jax.ShapeDtypeStruct((OWNERS, ROWS, WIDTH), LOW),
        scratch_shapes=[
            pltpu.VMEM((2, PULSES, 128), F32),
            pltpu.VMEM((2, PULSES, 128), F32),
            pltpu.VMEM((16, 256, 256), LOW),
            pltpu.VMEM((16, 256, 256), LOW),
            pltpu.VMEM((2, PULSES, 128), F32),
        ],
        name="azimuth_picture",
    )(received, received, phase, full, back, forward, backward)


def edge_kernel(mag, weights, full, back, forward, backward, out, xs, ys, vs, ms):
    spread_rows(mag, xs)

    def outer(p, _):
        ys[p] = dot(full[:, :128], pulse_rows(xs, p).astype(LOW)).astype(LOW)
        return 0

    lax.fori_loop(0, 16, outer, 0, unroll=4)

    def inner(g, _):
        rows = pl.ds(pl.multiple_of(g * 16, 16), 16)
        y = dot(forward[g], ys[:, rows, :].reshape(256, 256)).reshape(16, 2, 8, 256)
        w = weights[g]
        w = beside(w, w).reshape(16, 8, 256)
        z = jnp.stack([-y[:, 1] * w, y[:, 0] * w], 1).reshape(256, 256).astype(LOW)
        vs[:, rows, :] = dot(backward[g], z).astype(LOW).reshape(16, 16, 256)
        return 0

    lax.fori_loop(0, 16, inner, 0, unroll=2)

    def last(p, _):
        x = dot(back[:128, :], vs[p])
        at = pl.ds(p, 128, stride=ROWS)
        ms[0, at, :] = x[:, :128]
        ms[1, at, :] = x[:, 128:]
        return 0

    lax.fori_loop(0, 16, last, 0, unroll=4)

    def gather(n, _):
        rows = pl.ds(pl.multiple_of(n * 128, 128), 128)
        out[rows, :128] = ms[0, rows, :]
        out[rows, 128:] = ms[1, rows, :]
        return 0

    lax.fori_loop(0, 16, gather, 0)


def azimuth_edges(mag, weights, full, back, forward, backward):
    return pl.pallas_call(
        edge_kernel,
        grid=(2,),
        in_specs=[
            pl.BlockSpec((OWNERS, ROWS, 256), lambda i: (0, 0, i)),
            whole((16, 128, 128)),
            whole((256, 256)),
            whole((256, 256)),
            whole((16, 256, 256)),
            whole((16, 256, 256)),
        ],
        out_specs=pl.BlockSpec((PULSES, 256), lambda i: (0, i)),
        out_shape=jax.ShapeDtypeStruct((PULSES, WIDTH), F32),
        scratch_shapes=[
            pltpu.VMEM((2, PULSES, 128), F32),
            pltpu.VMEM((16, 256, 256), LOW),
            pltpu.VMEM((16, 256, 256), LOW),
            pltpu.VMEM((2, PULSES, 128), F32),
        ],
        name="azimuth_edges",
    )(mag, weights, full, back, forward, backward)


def concentrate_kernel(mag, weights, first, second, third, last, turns, out, xs, os):
    def spread(n, _):
        rows = pl.ds(pl.multiple_of(n * 128, 128), 128)
        for k in range(4):
            v = mag[pl.ds(n * 8, 8), :, k * 128 : k * 128 + 128].astype(F32)
            xs[k, rows, :] = v.reshape(128, 128)
        return 0

    lax.fori_loop(0, 16, spread, 0)
    top = lax.broadcasted_iota(jnp.int32, (128, 256), 0) == 0

    def one(p):
        at = pl.ds(p, 128, stride=ROWS)
        x = above(beside(xs[0, at, :], xs[1, at, :]), beside(xs[2, at, :], xs[3, at, :]))
        y = dot(first[...], x.astype(LOW))
        re, im = y[:128], y[128:]
        mirror = jnp.where(top[:16], im[:16], 0.0)
        im = jnp.where(top, 0.0, im)
        parts = [(re, im, slice(0, 128)), (mirror, jnp.zeros_like(mirror), slice(128, 144))]
        jumped = []
        for e, z in enumerate(forward_spectrum(parts, turns, second)):
            w = weights[:, e * 128 : e * 128 + 128]
            jumped.append(beside(-z[:, 128:] * w, z[:, :128] * w).astype(LOW))
        (r0, i0), (r1, i1) = back_section(jumped[0], jumped[1], turns, third)
        re, im = beside(r0, r1), beside(i0, i1)
        im = above(jnp.where(top[:8], re[128:136], im[:8]), im[8:128])
        e = dot(last[...], above(re[:128], im).astype(LOW))
        for o in range(2):
            for h in range(2):
                os[h, pl.ds(o * ROWS + p, 128, stride=2 * ROWS), :] = e[
                    o * 128 : o * 128 + 128, h * 128 : h * 128 + 128
                ]

    def pair(i, _):
        one(2 * i)
        one(2 * i + 1)
        return 0

    lax.fori_loop(0, ROWS // 2, pair, 0)

    def gather(n, _):
        for u in range(4):
            at = n * 4 + u
            rows = pl.ds(pl.multiple_of(at * ROWS, ROWS), ROWS)
            out[:, pl.ds(pl.multiple_of(at * 256, 256), 256)] = beside(os[0, rows, :], os[1, rows, :])
        return 0

    lax.fori_loop(0, 64, gather, 0)


def range_concentrate(mag, weights, first, second, third, last, turns):
    return pl.pallas_call(
        concentrate_kernel,
        out_shape=jax.ShapeDtypeStruct((ROWS, BINS), F32),
        scratch_shapes=[
            pltpu.VMEM((4, PULSES, 128), F32),
            pltpu.VMEM((2, 256 * ROWS, 128), F32),
        ],
        name="range_concentrate",
    )(mag, weights, first, second, third, last, turns)


def signed(freqs, length):
    return jnp.where(freqs < length // 2, freqs, freqs - length)


def split_grid(values):
    grid = values.reshape(128, 2, 256)
    return grid.transpose(2, 1, 0).reshape(256, 256)


def azimuth_phase(rates):
    freqs = jnp.arange(PULSES, dtype=jnp.int32).reshape(16, 16, 8).transpose(1, 0, 2)
    s = signed(freqs, PULSES).astype(F32).reshape(16, 128, 1) / PULSES
    angles = (s * s) * rates[None, None, :]
    return jnp.stack([jnp.cos(angles), jnp.sin(angles)])


def azimuth_weights(factors):
    freqs = jnp.arange(PULSES, dtype=jnp.int32)
    values = jnp.sign(signed(freqs, PULSES)).astype(F32) * factors
    values = values.reshape(16, 16, 8).transpose(1, 0, 2).reshape(16, 128, 1)
    return jnp.broadcast_to(values, (16, 128, 128))


def range_weights(factors):
    freqs = jnp.arange(BINS, dtype=jnp.int32)
    signs = jnp.sign(signed(freqs, BINS)).astype(F32)
    partner = jnp.roll(jnp.flip(factors), 1)
    inside = freqs % 128 != 0
    values = signs * jnp.where(inside, factors + partner, factors)
    return split_grid(values)[:144]


def expand(compact):
    row = lax.broadcasted_iota(jnp.int32, (1, 1, 8, 256), 2)
    lane = lax.broadcasted_iota(jnp.int32, (1, 1, 8, 256), 3)
    kept = jnp.where(lane % 8 == row, compact[:, :, None, :], jnp.zeros((), LOW))
    return kept.reshape(16, 256, 256)


def on_device(raw_pulses, range_phase, azimuth_rate, conc_azimuth, conc_range):
    first, second, third, fourth = range_tables()
    turns = jnp.asarray(range_turns(256))
    grid = split_grid(range_phase)
    phase = jnp.stack([jnp.cos(grid), jnp.sin(grid)])
    blocks = range_compress(raw_pulses, phase, (first, second, third, fourth), turns)
    received = lax.all_to_all(blocks, AXES, split_axis=0, concat_axis=0, tiled=True)
    full, back, forward, backward = azimuth_tables()
    forward, backward, _ = lax.optimization_barrier((forward, backward, conc_azimuth))
    forward, backward = expand(forward), expand(backward)
    turn = azimuth_phase(azimuth_rate)
    mag = azimuth_picture(received, turn, full, back, forward, backward)
    shared = lax.all_to_all(mag, AXES, split_axis=0, concat_axis=0, tiled=True)
    edge_azimuth = azimuth_edges(mag, azimuth_weights(conc_azimuth), full, back, forward, backward)
    real_first, real_last = real_range_tables()
    edge_range = range_concentrate(
        shared, range_weights(conc_range), real_first, second, third, real_last, turns
    )
    return (edge_azimuth, edge_range)


def solution(mesh):
    in_specs = (P(None, AXES, None), P(), P(AXES), P(), P())
    out_specs = (P(None, AXES), P(AXES, None))
    return jax.shard_map(
        on_device, mesh=mesh, in_specs=in_specs, out_specs=out_specs, check_vma=False
    )
```

```python
import math

import jax
import jax.numpy as jnp
import numpy as np
from jax import lax
from jax.experimental import pallas as pl
from jax.experimental.pallas import tpu as pltpu
from jax.sharding import PartitionSpec as P

AXES = ("rg", "az")
BINS = 65536
PULSES = 2048
ROWS = 16
PITCH = 18
FILLS = 4
OWNERS = 128
WIDTH = 512
LOW = jnp.bfloat16
F32 = jnp.float32


def roots(exponents, length):
    angles = 2.0 * math.pi / length * (exponents % length)
    return np.cos(angles) + 1j * np.sin(angles)


def left_form(matrix):
    return np.block([[matrix.real, -matrix.imag], [matrix.imag, matrix.real]])


def right_form(matrix):
    return np.block([[matrix.real, matrix.imag], [-matrix.imag, matrix.real]])


def low(table):
    return np.asarray(table, np.float32).astype(LOW)


def range_tables():
    k = np.arange(128)[:, None]
    j = np.arange(128)[None, :]
    even = roots(2 * j * k, 256) / 16.0
    odd = roots((2 * j + 1) * k, 256) / 16.0
    first = np.stack([left_form(even.conj()), left_form(odd.conj())])
    second = np.stack([right_form(even.conj()), right_form(odd.conj())])
    third = np.stack([right_form(even.T), right_form(odd.T)])
    fourth = np.stack([left_form(even.T), left_form(odd.T)])
    return tuple(low(t) for t in (first, second, third, fourth))


def range_turns(rows):
    table = roots(np.arange(rows)[:, None] * np.arange(256)[None, :], BINS)
    return np.stack([table.real, table.imag]).astype(np.float32)


def real_range_tables():
    k = np.arange(128)[:, None]
    n = np.concatenate([2 * np.arange(128), 2 * np.arange(128) + 1])[None, :]
    base = roots(k * n, 256) / 16.0
    mirror = np.cos(math.pi * n) / 16.0
    first = np.concatenate([base.real, mirror, -base.imag[1:]], 0)
    last = np.concatenate([base.real.T, mirror.T, -base.imag[1:].T], 1)
    return low(first), low(last)


def azimuth_tables():
    s = np.arange(128)
    outer = roots(-s[:, None] * s[None, :], 128) / math.sqrt(128.0)
    full = left_form(outer).reshape(2, 16, 8, 256).transpose(1, 0, 2, 3).reshape(256, 256)
    group = np.arange(16)[:, None, None, None]
    eight = np.arange(8)[None, None, None, :]
    fb = np.arange(16)[None, :, None, None]
    p = np.arange(16)[None, None, :, None]
    inner = roots(-p * (8 * group + eight + 128 * fb), PULSES) / 4.0
    pair = np.stack([np.stack([inner.real, -inner.imag], 3), np.stack([inner.imag, inner.real], 3)], 2)
    forward = pair.reshape(16, 32, 256)
    backward = pair.transpose(0, 3, 4, 1, 2, 5).reshape(16, 32, 256)
    return low(full), low(full.T), low(forward), low(backward)


def dot(a, b):
    return jnp.dot(a, b, preferred_element_type=F32)


def beside(a, b):
    return jnp.concatenate([a, b], 1)


def above(a, b):
    return jnp.concatenate([a, b], 0)


def whole(shape):
    return pl.BlockSpec(shape, lambda i: (0,) * len(shape), pipeline_mode=pl.Buffered(1))


def together(jobs):
    while jobs:
        jobs = [job for job in jobs if next(job, None) is not None]


def forward_spectrum(parts, turns, second):
    sums, gaps = [], []
    for re, im, rows in parts:
        c, s = turns[0, rows, :], turns[1, rows, :]
        tr = re * c + im * s
        ti = im * c - re * s
        sums.append(beside(tr[:, :128] + tr[:, 128:], ti[:, :128] + ti[:, 128:]).astype(LOW))
        gaps.append(beside(tr[:, :128] - tr[:, 128:], ti[:, :128] - ti[:, 128:]).astype(LOW))
    return (
        dot(jnp.concatenate(sums, 0), second[0]),
        dot(jnp.concatenate(gaps, 0), second[1]),
    )


def back_section(even, odd, turns, third):
    even = dot(even, third[0])
    odd = dot(odd, third[1])
    rows = even.shape[0]
    halves = []
    for h, b in enumerate((even + odd, even - odd)):
        c = turns[0, :rows, h * 128 : h * 128 + 128]
        s = turns[1, :rows, h * 128 : h * 128 + 128]
        re, im = b[:, :128], b[:, 128:]
        halves.append((re * c - im * s, re * s + im * c))
    return halves


def sine_cosine(x):
    t = 0.5 * x
    u = t * t
    s = 1.0 / 39916800.0
    for k in (362880.0, -5040.0, 120.0, -6.0, 1.0):
        s = 1.0 / k + u * s if k != 362880.0 else 1.0 / k - u * s
    s = s * t
    c = 1.0 / 479001600.0
    for k in (-3628800.0, 40320.0, -720.0, 24.0, -2.0, 1.0):
        c = 1.0 / k + u * c
    return 2.0 * s * c, 1.0 - 2.0 * s * s


def compress_kernel(raw, angles, first, second, third, fourth, turns, out, xs, os, phase):
    step = pl.program_id(0)

    @pl.when(step == 0)
    def _():
        sine, cosine = sine_cosine(angles[...].T)
        for e in range(2):
            phase[0, :, e * 128 : e * 128 + 128] = cosine[e * 256 : e * 256 + 256]
            phase[1, :, e * 128 : e * 128 + 128] = sine[e * 256 : e * 256 + 256]

    @pl.when(step < FILLS)
    def _():
        def spread(n, _):
            for u in range(4):
                at = n * 4 + u
                for c in range(2):
                    v = raw[c, :, pl.ds(pl.multiple_of(at * 256, 256), 256)].astype(F32)
                    row = (step * (256 // FILLS) + at) * PITCH
                    xs[c, 0, pl.ds(row, ROWS), :] = v[:, :128]
                    xs[c, 1, pl.ds(row, ROWS), :] = v[:, 128:]
            return 0

        lax.fori_loop(0, 64 // FILLS, spread, 0)

    @pl.when(step == FILLS - 1)
    def _():
        compress_pulses(first, second, third, fourth, turns, xs, os, phase)

    @pl.when(step >= FILLS)
    def _():
        def gather(n, _):
            for u in range(4):
                at = n * 4 + u
                row = ((step - FILLS) * (OWNERS // FILLS) + at) * PITCH
                for k in range(8):
                    v = os[k, pl.ds(row, ROWS), :].astype(LOW)
                    out[at, :, k * 128 : k * 128 + 128] = v
            return 0

        lax.fori_loop(0, OWNERS // FILLS // 4, gather, 0)


def compress_pulses(first, second, third, fourth, turns, xs, os, phase):
    def one(p):
        def load(odd):
            def half(c):
                at = pl.ds(odd * PITCH + p, 128, stride=2 * PITCH)
                return beside(xs[c, 0, at, :], xs[c, 1, at, :])

            return above(half(0), half(1)).astype(LOW)

        even = dot(first[0], load(0))
        odd = dot(first[1], load(1))
        yield 1
        lo, hi = even + odd, even - odd
        parts = [(v[:128], v[128:], slice(r, r + 128)) for v, r in ((lo, 0), (hi, 128))]
        turned = []
        for e, z in enumerate(forward_spectrum(parts, turns, second)):
            c = phase[0, :, e * 128 : e * 128 + 128]
            s = phase[1, :, e * 128 : e * 128 + 128]
            re, im = z[:, :128], z[:, 128:]
            turned.append(beside(re * c - im * s, re * s + im * c).astype(LOW))
        yield 1
        (r0, i0), (r1, i1) = back_section(turned[0], turned[1], turns, third)
        re, im = beside(r0, r1), beside(i0, i1)
        sums = above(re[:128] + re[128:], im[:128] + im[128:]).astype(LOW)
        gaps = above(re[:128] - re[128:], im[:128] - im[128:]).astype(LOW)
        yield 1
        for o, c in enumerate((dot(fourth[0], sums), dot(fourth[1], gaps))):
            for part in range(2):
                for h in range(2):
                    os[part * 4 + o * 2 + h, pl.ds(p, 128, stride=PITCH), :] = c[
                        part * 128 : part * 128 + 128, h * 128 : h * 128 + 128
                    ]

    def some(i, _):
        together([one(4 * i + u) for u in range(4)])
        return 0

    lax.fori_loop(0, ROWS // 4, some, 0)


def range_compress(raw, angles, tables, turns):
    return pl.pallas_call(
        compress_kernel,
        grid=(2 * FILLS,),
        in_specs=[
            pl.BlockSpec((2, ROWS, BINS // FILLS), lambda i: (0, 0, jnp.minimum(i, FILLS - 1))),
            whole((128, 512)),
            *[whole((2, 256, 256)) for _ in range(5)],
        ],
        out_specs=pl.BlockSpec(
            (OWNERS // FILLS, ROWS, 1024), lambda i: (jnp.maximum(i - FILLS, 0), 0, 0)
        ),
        out_shape=jax.ShapeDtypeStruct((OWNERS, ROWS, 1024), LOW),
        scratch_shapes=[
            pltpu.VMEM((2, 2, 256 * PITCH, 128), F32),
            pltpu.VMEM((8, OWNERS * PITCH, 128), F32),
            pltpu.VMEM((2, 256, 256), F32),
        ],
        name="range_compress",
    )(raw, angles, *tables, turns)


def spread_rows(source, xs):
    def move(n, _):
        for u in range(8):
            at = n * 8 + u
            for h in range(2):
                v = source[at, :, h * 128 : h * 128 + 128].astype(F32)
                xs[h, pl.ds(at * PITCH, ROWS), :] = v
        return 0

    lax.fori_loop(0, 16, move, 0)


def pulse_rows(xs, p):
    at = pl.ds(p, 128, stride=PITCH)
    return beside(xs[0, at, :], xs[1, at, :])


def picture_kernel(re, im, phase, full, back, forward, backward, out, xr, xi, ys, vs, ms):
    spread_rows(re, xr)
    spread_rows(im, xi)

    def outer(p, _):
        x = above(pulse_rows(xr, p), pulse_rows(xi, p)).astype(LOW)
        ys[p] = dot(full[...], x).astype(LOW)
        return 0

    lax.fori_loop(0, 16, outer, 0, unroll=8)

    def inner(g, _):
        rows = pl.ds(pl.multiple_of(g * 16, 16), 16)
        y = dot(forward[g], ys[:, rows, :].reshape(256, 256)).reshape(16, 2, 8, 256)
        c = phase[0, g].reshape(16, 8, 256)
        s = phase[1, g].reshape(16, 8, 256)
        zr = y[:, 0] * c - y[:, 1] * s
        zi = y[:, 0] * s + y[:, 1] * c
        z = jnp.stack([zr, zi], 1).reshape(256, 256).astype(LOW)
        vs[:, rows, :] = dot(backward[g], z).astype(LOW).reshape(16, 16, 256)
        return 0

    lax.fori_loop(0, 16, inner, 0, unroll=4)

    def last(p, _):
        x = dot(back[...], vs[p])
        a, b = x[:128], x[128:]
        m = jnp.sqrt(a * a + b * b)
        at = pl.ds(p, 128, stride=PITCH)
        ms[0, at, :] = m[:, :128]
        ms[1, at, :] = m[:, 128:]
        return 0

    lax.fori_loop(0, 16, last, 0, unroll=8)

    def gather(n, _):
        for u in range(8):
            at = n * 8 + u
            for h in range(2):
                v = ms[h, pl.ds(at * PITCH, ROWS), :].astype(LOW)
                out[at, :, h * 128 : h * 128 + 128] = v
        return 0

    lax.fori_loop(0, 16, gather, 0)


def azimuth_picture(received, phase, full, back, forward, backward):
    return pl.pallas_call(
        picture_kernel,
        grid=(2,),
        in_specs=[
            pl.BlockSpec((OWNERS, ROWS, 256), lambda i: (0, 0, i)),
            pl.BlockSpec((OWNERS, ROWS, 256), lambda i: (0, 0, i + 2)),
            pl.BlockSpec((2, 16, 128, 256), lambda i: (0, 0, 0, i)),
            whole((256, 256)),
            whole((256, 256)),
            whole((16, 256, 256)),
            whole((16, 256, 256)),
        ],
        out_specs=pl.BlockSpec((OWNERS, ROWS, 256), lambda i: (0, 0, i)),
        out_shape=jax.ShapeDtypeStruct((OWNERS, ROWS, WIDTH), LOW),
        scratch_shapes=[
            pltpu.VMEM((2, OWNERS * PITCH, 128), F32),
            pltpu.VMEM((2, OWNERS * PITCH, 128), F32),
            pltpu.VMEM((16, 256, 256), LOW),
            pltpu.VMEM((16, 256, 256), LOW),
            pltpu.VMEM((2, OWNERS * PITCH, 128), F32),
        ],
        name="azimuth_picture",
    )(received, received, phase, full, back, forward, backward)


def edge_kernel(mag, weights, full, back, forward, backward, out, xs, ys, vs, ms):
    spread_rows(mag, xs)

    def outer(p, _):
        ys[p] = dot(full[:, :128], pulse_rows(xs, p).astype(LOW)).astype(LOW)
        return 0

    lax.fori_loop(0, 16, outer, 0, unroll=4)

    def inner(g, _):
        rows = pl.ds(pl.multiple_of(g * 16, 16), 16)
        y = dot(forward[g], ys[:, rows, :].reshape(256, 256)).reshape(16, 2, 8, 256)
        w = weights[g]
        w = beside(w, w).reshape(16, 8, 256)
        z = jnp.stack([-y[:, 1] * w, y[:, 0] * w], 1).reshape(256, 256).astype(LOW)
        vs[:, rows, :] = dot(backward[g], z).astype(LOW).reshape(16, 16, 256)
        return 0

    lax.fori_loop(0, 16, inner, 0, unroll=2)

    def last(p, _):
        x = dot(back[:128, :], vs[p])
        at = pl.ds(p, 128, stride=PITCH)
        ms[0, at, :] = x[:, :128]
        ms[1, at, :] = x[:, 128:]
        return 0

    lax.fori_loop(0, 16, last, 0, unroll=4)

    def gather(n, _):
        for u in range(8):
            at = n * 8 + u
            rows = pl.ds(pl.multiple_of(at * ROWS, ROWS), ROWS)
            for h in range(2):
                out[rows, h * 128 : h * 128 + 128] = ms[h, pl.ds(at * PITCH, ROWS), :]
        return 0

    lax.fori_loop(0, 16, gather, 0)


def azimuth_edges(mag, weights, full, back, forward, backward):
    return pl.pallas_call(
        edge_kernel,
        grid=(2,),
        in_specs=[
            pl.BlockSpec((OWNERS, ROWS, 256), lambda i: (0, 0, i)),
            whole((16, 128, 128)),
            whole((256, 256)),
            whole((256, 256)),
            whole((16, 256, 256)),
            whole((16, 256, 256)),
        ],
        out_specs=pl.BlockSpec((PULSES, 256), lambda i: (0, i)),
        out_shape=jax.ShapeDtypeStruct((PULSES, WIDTH), F32),
        scratch_shapes=[
            pltpu.VMEM((2, OWNERS * PITCH, 128), F32),
            pltpu.VMEM((16, 256, 256), LOW),
            pltpu.VMEM((16, 256, 256), LOW),
            pltpu.VMEM((2, OWNERS * PITCH, 128), F32),
        ],
        name="azimuth_edges",
    )(mag, weights, full, back, forward, backward)


def concentrate_kernel(mag, weights, first, second, third, last, turns, out, xs, os):
    step = pl.program_id(0)

    @pl.when(step < 2)
    def _():
        def spread(n, _):
            for u in range(4):
                at = n * 4 + u
                for k in range(4):
                    v = mag[at, :, k * 128 : k * 128 + 128].astype(F32)
                    xs[k, pl.ds((step * (OWNERS // 2) + at) * PITCH, ROWS), :] = v
            return 0

        lax.fori_loop(0, OWNERS // 8, spread, 0)

    @pl.when(step == 1)
    def _():
        concentrate_pulses(weights, first, second, third, last, turns, xs, os)

    @pl.when(step >= 2)
    def _():
        def gather(n, _):
            for u in range(4):
                at = n * 4 + u
                rows = pl.ds(((step - 2) * (256 // FILLS) + at) * PITCH, ROWS)
                lanes = pl.ds(pl.multiple_of(at * 256, 256), 256)
                out[:, lanes] = beside(os[0, rows, :], os[1, rows, :])
            return 0

        lax.fori_loop(0, 64 // FILLS, gather, 0)


def concentrate_pulses(weights, first, second, third, last, turns, xs, os):
    top = lax.broadcasted_iota(jnp.int32, (128, 256), 0) == 0

    def one(p):
        at = pl.ds(p, 128, stride=PITCH)
        x = above(beside(xs[0, at, :], xs[1, at, :]), beside(xs[2, at, :], xs[3, at, :]))
        y = dot(first[...], x.astype(LOW))
        yield 1
        re, im = y[:128], y[128:]
        mirror = jnp.where(top[:16], im[:16], 0.0)
        im = jnp.where(top, 0.0, im)
        parts = [(re, im, slice(0, 128)), (mirror, jnp.zeros_like(mirror), slice(128, 144))]
        jumped = []
        for e, z in enumerate(forward_spectrum(parts, turns, second)):
            w = weights[:, e * 128 : e * 128 + 128]
            jumped.append(beside(-z[:, 128:] * w, z[:, :128] * w).astype(LOW))
        yield 1
        (r0, i0), (r1, i1) = back_section(jumped[0], jumped[1], turns, third)
        re, im = beside(r0, r1), beside(i0, i1)
        im = above(jnp.where(top[:8], re[128:136], im[:8]), im[8:128])
        yield 1
        e = dot(last[...], above(re[:128], im).astype(LOW))
        for o in range(2):
            for h in range(2):
                os[h, pl.ds(o * PITCH + p, 128, stride=2 * PITCH), :] = e[
                    o * 128 : o * 128 + 128, h * 128 : h * 128 + 128
                ]

    def some(i, _):
        together([one(4 * i + u) for u in range(4)])
        return 0

    lax.fori_loop(0, ROWS // 4, some, 0)


def range_concentrate(mag, weights, first, second, third, last, turns):
    return pl.pallas_call(
        concentrate_kernel,
        grid=(2 + FILLS,),
        in_specs=[
            pl.BlockSpec((OWNERS // 2, ROWS, WIDTH), lambda i: (jnp.minimum(i, 1), 0, 0)),
            whole((144, 256)),
            whole((256, 256)),
            whole((2, 256, 256)),
            whole((2, 256, 256)),
            whole((256, 256)),
            whole((2, 256, 256)),
        ],
        out_specs=pl.BlockSpec((ROWS, BINS // FILLS), lambda i: (0, jnp.maximum(i - 2, 0))),
        out_shape=jax.ShapeDtypeStruct((ROWS, BINS), F32),
        scratch_shapes=[
            pltpu.VMEM((4, OWNERS * PITCH, 128), F32),
            pltpu.VMEM((2, 256 * PITCH, 128), F32),
        ],
        compiler_params=pltpu.CompilerParams(vmem_limit_bytes=32 << 20),
        name="range_concentrate",
    )(mag, weights, first, second, third, last, turns)


def signed(freqs, length):
    return jnp.where(freqs < length // 2, freqs, freqs - length)


def split_grid(values):
    grid = values.reshape(128, 2, 256)
    return grid.transpose(2, 1, 0).reshape(256, 256)


def azimuth_phase(rates):
    freqs = jnp.arange(PULSES, dtype=jnp.int32).reshape(16, 16, 8).transpose(1, 0, 2)
    s = signed(freqs, PULSES).astype(F32).reshape(16, 128, 1) / PULSES
    angles = (s * s) * rates[None, None, :]
    return jnp.stack([jnp.cos(angles), jnp.sin(angles)])


def azimuth_weights(factors):
    freqs = jnp.arange(PULSES, dtype=jnp.int32)
    values = jnp.sign(signed(freqs, PULSES)).astype(F32) * factors
    values = values.reshape(16, 16, 8).transpose(1, 0, 2).reshape(16, 128, 1)
    return jnp.broadcast_to(values, (16, 128, 128))


def range_weights(factors):
    freqs = jnp.arange(BINS, dtype=jnp.int32)
    signs = jnp.sign(signed(freqs, BINS)).astype(F32)
    partner = jnp.roll(jnp.flip(factors), 1)
    inside = freqs % 128 != 0
    values = signs * jnp.where(inside, factors + partner, factors)
    return split_grid(values)[:144]


def expand(compact):
    row = lax.broadcasted_iota(jnp.int32, (1, 1, 8, 256), 2)
    lane = lax.broadcasted_iota(jnp.int32, (1, 1, 8, 256), 3)
    kept = jnp.where(lane % 8 == row, compact[:, :, None, :], jnp.zeros((), LOW))
    return kept.reshape(16, 256, 256)


def on_device(raw_pulses, range_phase, azimuth_rate, conc_azimuth, conc_range):
    first, second, third, fourth = range_tables()
    turns = jnp.asarray(range_turns(256))
    angles = range_phase.reshape(128, 512)
    blocks = range_compress(raw_pulses, angles, (first, second, third, fourth), turns)
    received = lax.all_to_all(blocks, AXES, split_axis=0, concat_axis=0, tiled=True)
    full, back, forward, backward = azimuth_tables()
    forward, backward, _ = lax.optimization_barrier((forward, backward, conc_azimuth))
    forward, backward = expand(forward), expand(backward)
    turn = azimuth_phase(azimuth_rate)
    mag = azimuth_picture(received, turn, full, back, forward, backward)
    shared = lax.all_to_all(mag, AXES, split_axis=0, concat_axis=0, tiled=True)
    edge_azimuth = azimuth_edges(mag, azimuth_weights(conc_azimuth), full, back, forward, backward)
    real_first, real_last = real_range_tables()
    edge_range = range_concentrate(
        shared, range_weights(conc_range), real_first, second, third, real_last, turns
    )
    return (edge_azimuth, edge_range)


def solution(mesh):
    in_specs = (P(None, AXES, None), P(), P(AXES), P(), P())
    out_specs = (P(None, AXES), P(AXES, None))
    return jax.shard_map(
        on_device, mesh=mesh, in_specs=in_specs, out_specs=out_specs, check_vma=False
    )
```

```python
import math

import jax
import jax.numpy as jnp
import numpy as np
from jax import lax
from jax.experimental import pallas as pl
from jax.experimental.pallas import tpu as pltpu
from jax.sharding import PartitionSpec as P

AXES = ("rg", "az")
BINS = 65536
PULSES = 2048
ROWS = 16
PITCH = 18
SMALLEST = float(np.finfo(np.float32).tiny)
FILLS = 4
OWNERS = 128
WIDTH = 512
LOW = jnp.bfloat16
F32 = jnp.float32


def roots(exponents, length):
    angles = 2.0 * math.pi / length * (exponents % length)
    return np.cos(angles) + 1j * np.sin(angles)


def left_form(matrix):
    return np.block([[matrix.real, -matrix.imag], [matrix.imag, matrix.real]])


def right_form(matrix):
    return np.block([[matrix.real, matrix.imag], [-matrix.imag, matrix.real]])


def low(table):
    return np.asarray(table, np.float32).astype(LOW)


def range_tables():
    k = np.arange(128)[:, None]
    j = np.arange(128)[None, :]
    even = roots(2 * j * k, 256) / 16.0
    odd = roots((2 * j + 1) * k, 256) / 16.0
    first = np.stack([left_form(even.conj()), left_form(odd.conj())])
    second = np.stack([right_form(even.conj()), right_form(odd.conj())])
    third = np.stack([right_form(even.T), right_form(odd.T)])
    fourth = np.stack([left_form(even.T), left_form(odd.T)])
    return tuple(low(t) for t in (first, second, third, fourth))


def range_turns(rows):
    table = roots(np.arange(rows)[:, None] * np.arange(256)[None, :], BINS)
    return np.stack([table.real, table.imag]).astype(np.float32)


def real_range_tables():
    k = np.arange(128)[:, None]
    n = np.concatenate([2 * np.arange(128), 2 * np.arange(128) + 1])[None, :]
    base = roots(k * n, 256) / 16.0
    mirror = np.cos(math.pi * n) / 16.0
    first = np.concatenate([base.real, mirror, -base.imag[1:]], 0)
    last = np.concatenate([base.real.T, mirror.T, -base.imag[1:].T], 1)
    return low(first), low(last)


def azimuth_tables():
    s = np.arange(128)
    outer = roots(-s[:, None] * s[None, :], 128) / math.sqrt(128.0)
    full = left_form(outer).reshape(2, 16, 8, 256).transpose(1, 0, 2, 3).reshape(256, 256)
    group = np.arange(16)[:, None, None, None]
    eight = np.arange(8)[None, None, None, :]
    fb = np.arange(16)[None, :, None, None]
    p = np.arange(16)[None, None, :, None]
    inner = roots(-p * (8 * group + eight + 128 * fb), PULSES) / 4.0
    pair = np.stack([np.stack([inner.real, -inner.imag], 3), np.stack([inner.imag, inner.real], 3)], 2)
    forward = pair.reshape(16, 32, 256)
    backward = pair.transpose(0, 3, 4, 1, 2, 5).reshape(16, 32, 256)
    return low(full), low(full.T), low(forward), low(backward)


def dot(a, b):
    return jnp.dot(a, b, preferred_element_type=F32)


def beside(a, b):
    return jnp.concatenate([a, b], 1)


def above(a, b):
    return jnp.concatenate([a, b], 0)


def whole(shape):
    return pl.BlockSpec(shape, lambda i: (0,) * len(shape), pipeline_mode=pl.Buffered(1))


def together(jobs):
    while jobs:
        jobs = [job for job in jobs if next(job, None) is not None]


def forward_spectrum(parts, turns, second):
    sums, gaps = [], []
    for re, im, rows in parts:
        c, s = turns[0, rows, :], turns[1, rows, :]
        tr = re * c + im * s
        ti = im * c - re * s
        sums.append(beside(tr[:, :128] + tr[:, 128:], ti[:, :128] + ti[:, 128:]).astype(LOW))
        gaps.append(beside(tr[:, :128] - tr[:, 128:], ti[:, :128] - ti[:, 128:]).astype(LOW))
    return (
        dot(jnp.concatenate(sums, 0), second[0]),
        dot(jnp.concatenate(gaps, 0), second[1]),
    )


def back_section(even, odd, turns, third):
    even = dot(even, third[0])
    odd = dot(odd, third[1])
    rows = even.shape[0]
    halves = []
    for h, b in enumerate((even + odd, even - odd)):
        c = turns[0, :rows, h * 128 : h * 128 + 128]
        s = turns[1, :rows, h * 128 : h * 128 + 128]
        re, im = b[:, :128], b[:, 128:]
        halves.append((re * c - im * s, re * s + im * c))
    return halves


def sine_cosine(x):
    t = 0.5 * x
    u = t * t
    s = 1.0 / 39916800.0
    for k in (362880.0, -5040.0, 120.0, -6.0, 1.0):
        s = 1.0 / k + u * s if k != 362880.0 else 1.0 / k - u * s
    s = s * t
    c = 1.0 / 479001600.0
    for k in (-3628800.0, 40320.0, -720.0, 24.0, -2.0, 1.0):
        c = 1.0 / k + u * c
    return 2.0 * s * c, 1.0 - 2.0 * s * s


def compress_kernel(raw, angles, first, second, third, fourth, turns, out, xs, os, phase):
    step = pl.program_id(0)

    @pl.when(step == 0)
    def _():
        for e in range(2):
            for h in range(2):
                part = angles[pl.ds(2 * e + h, 128, stride=4), :]
                sine, cosine = sine_cosine(part.T)
                phase[0, h * 128 : h * 128 + 128, e * 128 : e * 128 + 128] = cosine
                phase[1, h * 128 : h * 128 + 128, e * 128 : e * 128 + 128] = sine

    @pl.when(step < FILLS)
    def _():
        def spread(n, _):
            for u in range(8):
                at = n * 8 + u
                for c in range(2):
                    v = raw[c, :, pl.ds(pl.multiple_of(at * 256, 256), 256)].astype(F32)
                    row = (step * (256 // FILLS) + at) * PITCH
                    xs[c, 0, pl.ds(row, ROWS), :] = v[:, :128]
                    xs[c, 1, pl.ds(row, ROWS), :] = v[:, 128:]
            return 0

        lax.fori_loop(0, 32 // FILLS, spread, 0)

    @pl.when(step == FILLS - 1)
    def _():
        compress_pulses(first, second, third, fourth, turns, xs, os, phase)

    @pl.when(step >= FILLS)
    def _():
        def gather(n, _):
            for u in range(4):
                at = n * 4 + u
                row = ((step - FILLS) * (OWNERS // FILLS) + at) * PITCH
                for k in range(8):
                    v = os[k, pl.ds(row, ROWS), :].astype(LOW)
                    out[at, k] = v
            return 0

        lax.fori_loop(0, OWNERS // FILLS // 4, gather, 0)


def compress_pulses(first, second, third, fourth, turns, xs, os, phase):
    def one(p):
        def load(odd):
            def half(c):
                at = pl.ds(odd * PITCH + p, 128, stride=2 * PITCH)
                return beside(xs[c, 0, at, :], xs[c, 1, at, :])

            return above(half(0), half(1)).astype(LOW)

        even = dot(first[0], load(0))
        odd = dot(first[1], load(1))
        yield 1
        lo, hi = even + odd, even - odd
        parts = [(v[:128], v[128:], slice(r, r + 128)) for v, r in ((lo, 0), (hi, 128))]
        turned = []
        for e, z in enumerate(forward_spectrum(parts, turns, second)):
            c = phase[0, :, e * 128 : e * 128 + 128]
            s = phase[1, :, e * 128 : e * 128 + 128]
            re, im = z[:, :128], z[:, 128:]
            turned.append(beside(re * c - im * s, re * s + im * c).astype(LOW))
        yield 1
        (r0, i0), (r1, i1) = back_section(turned[0], turned[1], turns, third)
        re, im = beside(r0, r1), beside(i0, i1)
        sums = above(re[:128] + re[128:], im[:128] + im[128:]).astype(LOW)
        gaps = above(re[:128] - re[128:], im[:128] - im[128:]).astype(LOW)
        yield 1
        for o, c in enumerate((dot(fourth[0], sums), dot(fourth[1], gaps))):
            for part in range(2):
                for h in range(2):
                    os[part * 4 + o * 2 + h, pl.ds(p, 128, stride=PITCH), :] = c[
                        part * 128 : part * 128 + 128, h * 128 : h * 128 + 128
                    ]

    def some(i, _):
        together([one(4 * i + u) for u in range(4)])
        return 0

    lax.fori_loop(0, ROWS // 4, some, 0)


def range_compress(raw, angles, tables, turns):
    return pl.pallas_call(
        compress_kernel,
        grid=(2 * FILLS,),
        in_specs=[
            pl.BlockSpec((2, ROWS, BINS // FILLS), lambda i: (0, 0, jnp.minimum(i, FILLS - 1))),
            whole((512, 128)),
            *[whole((2, 256, 256)) for _ in range(5)],
        ],
        out_specs=pl.BlockSpec(
            (OWNERS // FILLS, 8, ROWS, 128), lambda i: (jnp.maximum(i - FILLS, 0), 0, 0, 0)
        ),
        out_shape=jax.ShapeDtypeStruct((OWNERS, 8, ROWS, 128), LOW),
        scratch_shapes=[
            pltpu.VMEM((2, 2, 256 * PITCH, 128), F32),
            pltpu.VMEM((8, OWNERS * PITCH, 128), F32),
            pltpu.VMEM((2, 256, 256), F32),
        ],
        name="range_compress",
    )(raw, angles, *tables, turns)


def spread_rows(source, xs):
    def move(n, _):
        for u in range(8):
            at = n * 8 + u
            for h in range(2):
                v = source[at, h].astype(F32)
                xs[h, pl.ds(at * PITCH, ROWS), :] = v
        return 0

    lax.fori_loop(0, 16, move, 0)


def pulse_rows(xs, p):
    at = pl.ds(p, 128, stride=PITCH)
    return beside(xs[0, at, :], xs[1, at, :])


def picture_kernel(
    re, im, cosine_far, sine_far, full, back, forward_far, backward_far, out,
    xr, xi, ys, vs, ms, cosine, sine, forward, backward, arrived,
):
    step = pl.program_id(0)
    tables = [
        pltpu.make_async_copy(forward_far, forward, arrived.at[0]),
        pltpu.make_async_copy(cosine_far.at[0], cosine.at[0], arrived.at[1]),
        pltpu.make_async_copy(sine_far.at[0], sine.at[0], arrived.at[2]),
        pltpu.make_async_copy(backward_far, backward, arrived.at[3]),
        pltpu.make_async_copy(cosine_far.at[1], cosine.at[1], arrived.at[4]),
        pltpu.make_async_copy(sine_far.at[1], sine.at[1], arrived.at[5]),
    ]

    @pl.when(step == 0)
    def _():
        for table in tables:
            table.start()

    spread_rows(re, xr)
    spread_rows(im, xi)

    def outer(p, _):
        x = above(pulse_rows(xr, p), pulse_rows(xi, p)).astype(LOW)
        ys[p] = dot(full[...], x).astype(LOW)
        return 0

    lax.fori_loop(0, 16, outer, 0, unroll=8)

    @pl.when(step == 0)
    def _():
        for table in tables[:4]:
            table.wait()

    @pl.when(step == 1)
    def _():
        for table in tables[4:]:
            table.wait()

    def inner(g, _):
        rows = pl.ds(pl.multiple_of(g * 16, 16), 16)
        y = dot(forward[g], ys[:, rows, :].reshape(256, 256)).reshape(16, 2, 8, 256)
        c = cosine[step, g].reshape(16, 8, 256)
        s = sine[step, g].reshape(16, 8, 256)
        zr = y[:, 0] * c - y[:, 1] * s
        zi = y[:, 0] * s + y[:, 1] * c
        z = jnp.stack([zr, zi], 1).reshape(256, 256).astype(LOW)
        vs[:, rows, :] = dot(backward[g], z).astype(LOW).reshape(16, 16, 256)
        return 0

    lax.fori_loop(0, 16, inner, 0, unroll=4)

    def last(p, _):
        x = dot(back[...], vs[p])
        a, b = x[:128], x[128:]
        m = a * a + b * b
        m = m * lax.rsqrt(jnp.maximum(m, SMALLEST))
        at = pl.ds(p, 128, stride=PITCH)
        ms[0, at, :] = m[:, :128]
        ms[1, at, :] = m[:, 128:]
        return 0

    lax.fori_loop(0, 16, last, 0, unroll=8)

    def gather(n, _):
        for u in range(8):
            at = n * 8 + u
            for h in range(2):
                out[at, h] = ms[h, pl.ds(at * PITCH, ROWS), :].astype(LOW)
        return 0

    lax.fori_loop(0, 16, gather, 0)


def azimuth_picture(received, cosine, sine, full, back, forward, backward):
    return pl.pallas_call(
        picture_kernel,
        grid=(2,),
        in_specs=[
            pl.BlockSpec((OWNERS, 2, ROWS, 128), lambda i: (0, i, 0, 0)),
            pl.BlockSpec((OWNERS, 2, ROWS, 128), lambda i: (0, i + 2, 0, 0)),
            pl.BlockSpec(memory_space=pltpu.HBM),
            pl.BlockSpec(memory_space=pltpu.HBM),
            whole((256, 256)),
            whole((256, 256)),
            pl.BlockSpec(memory_space=pltpu.HBM),
            pl.BlockSpec(memory_space=pltpu.HBM),
        ],
        out_specs=pl.BlockSpec((OWNERS, 2, ROWS, 128), lambda i: (0, i, 0, 0)),
        out_shape=pltpu.HBM((OWNERS, 4, ROWS, 128), LOW),
        scratch_shapes=[
            pltpu.VMEM((2, OWNERS * PITCH, 128), F32),
            pltpu.VMEM((2, OWNERS * PITCH, 128), F32),
            pltpu.VMEM((16, 256, 256), LOW),
            pltpu.VMEM((16, 256, 256), LOW),
            pltpu.VMEM((2, OWNERS * PITCH, 128), F32),
            pltpu.VMEM((2, 16, 128, 256), F32),
            pltpu.VMEM((2, 16, 128, 256), F32),
            pltpu.VMEM((16, 256, 256), LOW),
            pltpu.VMEM((16, 256, 256), LOW),
            pltpu.SemaphoreType.DMA((6,)),
        ],
        name="azimuth_picture",
    )(received, received, cosine, sine, full, back, forward, backward)


def edge_kernel(mag, weights, full, back, forward, backward, out, xs, ys, vs, ms):
    spread_rows(mag, xs)

    def outer(p, _):
        ys[p] = dot(full[:, :128], pulse_rows(xs, p).astype(LOW)).astype(LOW)
        return 0

    lax.fori_loop(0, 16, outer, 0, unroll=4)

    def inner(g, _):
        rows = pl.ds(pl.multiple_of(g * 16, 16), 16)
        y = dot(forward[g], ys[:, rows, :].reshape(256, 256)).reshape(16, 2, 8, 256)
        w = weights[g]
        w = beside(w, w).reshape(16, 8, 256)
        z = jnp.stack([-y[:, 1] * w, y[:, 0] * w], 1).reshape(256, 256).astype(LOW)
        vs[:, rows, :] = dot(backward[g], z).astype(LOW).reshape(16, 16, 256)
        return 0

    lax.fori_loop(0, 16, inner, 0, unroll=2)

    def last(p, _):
        x = dot(back[:128, :], vs[p])
        at = pl.ds(p, 128, stride=PITCH)
        ms[0, at, :] = x[:, :128]
        ms[1, at, :] = x[:, 128:]
        return 0

    lax.fori_loop(0, 16, last, 0, unroll=4)

    def gather(n, _):
        for u in range(8):
            at = n * 8 + u
            rows = pl.ds(pl.multiple_of(at * ROWS, ROWS), ROWS)
            for h in range(2):
                out[rows, h * 128 : h * 128 + 128] = ms[h, pl.ds(at * PITCH, ROWS), :]
        return 0

    lax.fori_loop(0, 16, gather, 0)


def azimuth_edges(mag, weights, full, back, forward, backward):
    return pl.pallas_call(
        edge_kernel,
        grid=(2,),
        in_specs=[
            pl.BlockSpec((OWNERS, 2, ROWS, 128), lambda i: (0, i, 0, 0)),
            whole((16, 128, 128)),
            whole((256, 256)),
            whole((256, 256)),
            whole((16, 256, 256)),
            whole((16, 256, 256)),
        ],
        out_specs=pl.BlockSpec((PULSES, 256), lambda i: (0, i)),
        out_shape=jax.ShapeDtypeStruct((PULSES, WIDTH), F32),
        scratch_shapes=[
            pltpu.VMEM((2, OWNERS * PITCH, 128), F32),
            pltpu.VMEM((16, 256, 256), LOW),
            pltpu.VMEM((16, 256, 256), LOW),
            pltpu.VMEM((2, OWNERS * PITCH, 128), F32),
        ],
        name="azimuth_edges",
    )(mag, weights, full, back, forward, backward)


def concentrate_kernel(mag, weights, first, second, third, last, turns, out, xs, os):
    step = pl.program_id(0)

    @pl.when(step < 2)
    def _():
        def spread(n, _):
            for u in range(4):
                at = n * 4 + u
                for k in range(4):
                    v = mag[at, k].astype(F32)
                    xs[k, pl.ds((step * (OWNERS // 2) + at) * PITCH, ROWS), :] = v
            return 0

        lax.fori_loop(0, OWNERS // 8, spread, 0)

    @pl.when(step == 1)
    def _():
        concentrate_pulses(weights, first, second, third, last, turns, xs, os)

    @pl.when(step >= 2)
    def _():
        def gather(n, _):
            for u in range(4):
                at = n * 4 + u
                rows = pl.ds(((step - 2) * (256 // FILLS) + at) * PITCH, ROWS)
                lanes = pl.ds(pl.multiple_of(at * 256, 256), 256)
                out[:, lanes] = beside(os[0, rows, :], os[1, rows, :])
            return 0

        lax.fori_loop(0, 64 // FILLS, gather, 0)


def concentrate_pulses(weights, first, second, third, last, turns, xs, os):
    top = lax.broadcasted_iota(jnp.int32, (128, 256), 0) == 0

    def one(p):
        at = pl.ds(p, 128, stride=PITCH)
        x = above(beside(xs[0, at, :], xs[1, at, :]), beside(xs[2, at, :], xs[3, at, :]))
        y = dot(first[...], x.astype(LOW))
        yield 1
        re, im = y[:128], y[128:]
        mirror = jnp.where(top[:16], im[:16], 0.0)
        im = jnp.where(top, 0.0, im)
        parts = [(re, im, slice(0, 128)), (mirror, jnp.zeros_like(mirror), slice(128, 144))]
        jumped = []
        for e, z in enumerate(forward_spectrum(parts, turns, second)):
            w = weights[:, e * 128 : e * 128 + 128]
            jumped.append(beside(-z[:, 128:] * w, z[:, :128] * w).astype(LOW))
        yield 1
        (r0, i0), (r1, i1) = back_section(jumped[0], jumped[1], turns, third)
        re, im = beside(r0, r1), beside(i0, i1)
        im = above(jnp.where(top[:8], re[128:136], im[:8]), im[8:128])
        yield 1
        e = dot(last[...], above(re[:128], im).astype(LOW))
        for o in range(2):
            for h in range(2):
                os[h, pl.ds(o * PITCH + p, 128, stride=2 * PITCH), :] = e[
                    o * 128 : o * 128 + 128, h * 128 : h * 128 + 128
                ]

    def some(i, _):
        together([one(4 * i + u) for u in range(4)])
        return 0

    lax.fori_loop(0, ROWS // 4, some, 0)


def range_concentrate(mag, weights, first, second, third, last, turns):
    return pl.pallas_call(
        concentrate_kernel,
        grid=(2 + FILLS,),
        in_specs=[
            pl.BlockSpec((OWNERS // 2, 4, ROWS, 128), lambda i: (jnp.minimum(i, 1), 0, 0, 0)),
            whole((144, 256)),
            whole((256, 256)),
            whole((2, 256, 256)),
            whole((2, 256, 256)),
            whole((256, 256)),
            whole((2, 256, 256)),
        ],
        out_specs=pl.BlockSpec((ROWS, BINS // FILLS), lambda i: (0, jnp.maximum(i - 2, 0))),
        out_shape=jax.ShapeDtypeStruct((ROWS, BINS), F32),
        scratch_shapes=[
            pltpu.VMEM((4, OWNERS * PITCH, 128), F32),
            pltpu.VMEM((2, 256 * PITCH, 128), F32),
        ],
        compiler_params=pltpu.CompilerParams(vmem_limit_bytes=32 << 20),
        name="range_concentrate",
    )(mag, weights, first, second, third, last, turns)


def signed(freqs, length):
    return jnp.where(freqs < length // 2, freqs, freqs - length)


def split_grid(values):
    grid = values.reshape(128, 2, 256)
    return grid.transpose(2, 1, 0).reshape(256, 256)


def azimuth_phase(rates):
    freqs = jnp.arange(PULSES, dtype=jnp.int32).reshape(16, 16, 8).transpose(1, 0, 2)
    s = signed(freqs, PULSES).astype(F32).reshape(1, 16, 128, 1) / PULSES
    angles = (s * s) * rates.reshape(2, 1, 1, 256)
    return jnp.cos(angles), jnp.sin(angles)


def azimuth_weights(factors):
    freqs = jnp.arange(PULSES, dtype=jnp.int32)
    values = jnp.sign(signed(freqs, PULSES)).astype(F32) * factors
    values = values.reshape(16, 16, 8).transpose(1, 0, 2).reshape(16, 128, 1)
    return jnp.broadcast_to(values, (16, 128, 128))


def range_weights(factors):
    freqs = jnp.arange(BINS, dtype=jnp.int32)
    signs = jnp.sign(signed(freqs, BINS)).astype(F32)
    partner = jnp.roll(jnp.flip(factors), 1)
    inside = freqs % 128 != 0
    values = signs * jnp.where(inside, factors + partner, factors)
    return split_grid(values)[:144]


def expand(compact):
    row = lax.broadcasted_iota(jnp.int32, (1, 1, 8, 256), 2)
    lane = lax.broadcasted_iota(jnp.int32, (1, 1, 8, 256), 3)
    kept = jnp.where(lane % 8 == row, compact[:, :, None, :], jnp.zeros((), LOW))
    return kept.reshape(16, 256, 256)


def on_device(raw_pulses, range_phase, azimuth_rate, conc_azimuth, conc_range):
    first, second, third, fourth = range_tables()
    turns = jnp.asarray(range_turns(256))
    angles = range_phase.reshape(512, 128)
    blocks = range_compress(raw_pulses, angles, (first, second, third, fourth), turns)
    received = lax.all_to_all(blocks, AXES, split_axis=0, concat_axis=0, tiled=True)
    full, back, forward, backward = azimuth_tables()
    forward, backward, _ = lax.optimization_barrier((forward, backward, conc_azimuth))
    forward, backward = expand(forward), expand(backward)
    cosine, sine = azimuth_phase(azimuth_rate)
    mag = azimuth_picture(received, cosine, sine, full, back, forward, backward)
    shared = lax.all_to_all(mag, AXES, split_axis=0, concat_axis=0, tiled=True)
    edge_azimuth = azimuth_edges(mag, azimuth_weights(conc_azimuth), full, back, forward, backward)
    real_first, real_last = real_range_tables()
    edge_range = range_concentrate(
        shared, range_weights(conc_range), real_first, second, third, real_last, turns
    )
    return (edge_azimuth, edge_range)


def solution(mesh):
    in_specs = (P(None, AXES, None), P(), P(AXES), P(), P())
    out_specs = (P(None, AXES), P(AXES, None))
    return jax.shard_map(
        on_device, mesh=mesh, in_specs=in_specs, out_specs=out_specs, check_vma=False
    )
```

```python
import math

import jax
import jax.numpy as jnp
import numpy as np
from jax import lax
from jax.experimental import pallas as pl
from jax.experimental.pallas import tpu as pltpu
from jax.sharding import PartitionSpec as P

AXES = ("rg", "az")
BINS = 65536
PULSES = 2048
ROWS = 16
PITCH = 18
SMALLEST = float(np.finfo(np.float32).tiny)
FILLS = 4
OWNERS = 128
WIDTH = 512
LOW = jnp.bfloat16
F32 = jnp.float32


def roots(exponents, length):
    angles = 2.0 * math.pi / length * (exponents % length)
    return np.cos(angles) + 1j * np.sin(angles)


def left_form(matrix):
    return np.block([[matrix.real, -matrix.imag], [matrix.imag, matrix.real]])


def right_form(matrix):
    return np.block([[matrix.real, matrix.imag], [-matrix.imag, matrix.real]])


def paired(matrix):
    return matrix.reshape(2, 16, 8, -1).transpose(1, 0, 2, 3).reshape(256, -1)


def low(table):
    return np.asarray(table, np.float32).astype(LOW)


def range_tables():
    k = np.arange(128)[:, None]
    j = np.arange(128)[None, :]
    even = roots(2 * j * k, 256) / 16.0
    odd = roots((2 * j + 1) * k, 256) / 16.0
    first = np.stack([paired(left_form(even.conj())), paired(left_form(odd.conj()))])
    second = np.stack([right_form(even.conj()), right_form(odd.conj())])
    third = np.stack([right_form(even.T), right_form(odd.T)])
    fourth = np.stack([left_form(even.T), left_form(odd.T)])
    return tuple(low(t) for t in (first, second, third, fourth))


def range_turns():
    table = paired(roots(np.arange(256)[:, None] * np.arange(256)[None, :], BINS))
    return np.stack([table.real, table.imag]).astype(np.float32)


def real_range_tables():
    k = np.arange(128)[:, None]
    n = np.concatenate([2 * np.arange(128), 2 * np.arange(128) + 1])[None, :]
    base = roots(k * n, 256) / 16.0
    mirror = np.cos(math.pi * n) / 16.0
    first = np.concatenate([base.real, mirror, -base.imag[1:]], 0)
    last = np.concatenate([base.real.T, mirror.T, -base.imag[1:].T], 1)
    return low(paired(first)), low(last)


def azimuth_tables():
    s = np.arange(128)
    outer = roots(-s[:, None] * s[None, :], 128) / math.sqrt(128.0)
    full = paired(left_form(outer))
    group = np.arange(16)[:, None, None, None]
    eight = np.arange(8)[None, None, None, :]
    fb = np.arange(16)[None, :, None, None]
    p = np.arange(16)[None, None, :, None]
    inner = roots(-p * (8 * group + eight + 128 * fb), PULSES) / 4.0
    pair = np.stack([np.stack([inner.real, -inner.imag], 3), np.stack([inner.imag, inner.real], 3)], 2)
    forward = pair.reshape(16, 32, 256)
    backward = pair.transpose(0, 3, 4, 1, 2, 5).reshape(16, 32, 256)
    return low(full), low(paired(full.T)), low(full.T[:128]), low(forward), low(backward)


def dot(a, b):
    return jnp.dot(a, b, preferred_element_type=F32)


def beside(a, b):
    return jnp.concatenate([a, b], 1)


def above(a, b):
    return jnp.concatenate([a, b], 0)


def whole(shape):
    return pl.BlockSpec(shape, lambda i: (0,) * len(shape), pipeline_mode=pl.Buffered(1))


def together(jobs):
    asked = [next(job) for job in jobs]
    while asked:
        sent = [None] * len(jobs)
        if asked[0] is not None:
            rows = asked[0][0].shape[0]
            results = []
            for e in range(2):
                lhs = jnp.concatenate([ask[e] for ask in asked], 0)
                results.append(dot(lhs, asked[0][2][e]))
            sent = [[r[n * rows : n * rows + rows] for r in results] for n in range(len(jobs))]
        nexts = []
        for job, value in zip(jobs, sent):
            try:
                nexts.append(job.send(value))
            except StopIteration:
                pass
        asked = nexts


def groups(value):
    return value.reshape(-1, 2, 8, value.shape[-1])


def halves(value):
    return value[..., :128], value[..., 128:]


def flat(value):
    return value.reshape(-1, value.shape[-1])


def turned_back(re, im, c, s):
    return re * c + im * s, im * c - re * s


def turned_on(re, im, c, s):
    return re * c - im * s, re * s + im * c


def sum_and_gap(re, im):
    (r0, r1), (i0, i1) = halves(re), halves(im)
    join = lambda a, b: jnp.concatenate([a, b], -1)
    return join(r0 + r1, i0 + i1), join(r0 - r1, i0 - i1)


def sine_cosine(x):
    t = 0.5 * x
    u = t * t
    s = 1.0 / 39916800.0
    for k in (362880.0, -5040.0, 120.0, -6.0, 1.0):
        s = 1.0 / k + u * s if k != 362880.0 else 1.0 / k - u * s
    s = s * t
    c = 1.0 / 479001600.0
    for k in (-3628800.0, 40320.0, -720.0, 24.0, -2.0, 1.0):
        c = 1.0 / k + u * c
    return 2.0 * s * c, 1.0 - 2.0 * s * s


def compress_kernel(raw, angles, first, second, third, fourth, turns, out, xs, os, phase):
    step = pl.program_id(0)

    @pl.when(step == 0)
    def _():
        for e in range(2):
            for h in range(2):
                part = angles[pl.ds(2 * e + h, 128, stride=4), :]
                sine, cosine = sine_cosine(part.T)
                for t in range(16):
                    rows = slice(t * 16 + h * 8, t * 16 + h * 8 + 8)
                    phase[0, rows, e * 128 : e * 128 + 128] = cosine[t * 8 : t * 8 + 8]
                    phase[1, rows, e * 128 : e * 128 + 128] = sine[t * 8 : t * 8 + 8]

    @pl.when(step < FILLS)
    def _():
        def spread(n, _):
            for u in range(8):
                at = n * 8 + u
                for c in range(2):
                    v = raw[c, :, pl.ds(pl.multiple_of(at * 256, 256), 256)].astype(F32)
                    row = (step * (256 // FILLS) + at) * PITCH
                    xs[c, 0, pl.ds(row, ROWS), :] = v[:, :128]
                    xs[c, 1, pl.ds(row, ROWS), :] = v[:, 128:]
            return 0

        lax.fori_loop(0, 32 // FILLS, spread, 0)

    @pl.when(step == FILLS - 1)
    def _():
        compress_pulses(first, second, third, fourth, turns, xs, os, phase)

    @pl.when(step >= FILLS)
    def _():
        def gather(n, _):
            for u in range(4):
                at = n * 4 + u
                row = ((step - FILLS) * (OWNERS // FILLS) + at) * PITCH
                for k in range(8):
                    v = os[k, pl.ds(row, ROWS), :].astype(LOW)
                    out[at, k] = v
            return 0

        lax.fori_loop(0, OWNERS // FILLS // 4, gather, 0)


def compress_pulses(first, second, third, fourth, turns, xs, os, phase):
    def one(p):
        def load(odd):
            def half(c):
                at = pl.ds(odd * PITCH + p, 128, stride=2 * PITCH)
                return beside(xs[c, 0, at, :], xs[c, 1, at, :])

            return above(half(0), half(1)).astype(LOW)

        even = groups(dot(first[0], load(0)))
        odd = groups(dot(first[1], load(1)))
        yield
        c, s = groups(turns[0]), groups(turns[1])
        parts = []
        for h, v in enumerate((even + odd, even - odd)):
            parts.append(sum_and_gap(*turned_back(v[:, 0], v[:, 1], c[:, h], s[:, h])))
        zs = [flat(jnp.stack([parts[0][e], parts[1][e]], 1)).astype(LOW) for e in range(2)]
        zs = yield (zs[0], zs[1], second)
        turned = []
        for e in range(2):
            re, im = halves(zs[e])
            at = slice(e * 128, e * 128 + 128)
            turned.append(beside(*turned_on(re, im, phase[0, :, at], phase[1, :, at])).astype(LOW))
        even, odd = yield (turned[0], turned[1], third)
        even, odd = groups(even), groups(odd)
        sums, gaps = [], []
        for h, b in enumerate((even + odd, even - odd)):
            at = slice(h * 128, h * 128 + 128)
            re, im = halves(b)
            re, im = turned_on(re, im, groups(turns[0])[..., at], groups(turns[1])[..., at])
            sums.append((flat(re[:, 0] + re[:, 1]), flat(im[:, 0] + im[:, 1])))
            gaps.append((flat(re[:, 0] - re[:, 1]), flat(im[:, 0] - im[:, 1])))
        sums, gaps = (
            above(beside(v[0][0], v[1][0]), beside(v[0][1], v[1][1])).astype(LOW)
            for v in (sums, gaps)
        )
        yield
        for o, c in enumerate((dot(fourth[0], sums), dot(fourth[1], gaps))):
            for part in range(2):
                for h in range(2):
                    os[part * 4 + o * 2 + h, pl.ds(p, 128, stride=PITCH), :] = c[
                        part * 128 : part * 128 + 128, h * 128 : h * 128 + 128
                    ]

    def some(i, _):
        together([one(4 * i + u) for u in range(4)])
        return 0

    lax.fori_loop(0, ROWS // 4, some, 0)


def range_compress(raw, angles, tables, turns):
    return pl.pallas_call(
        compress_kernel,
        grid=(2 * FILLS,),
        in_specs=[
            pl.BlockSpec((2, ROWS, BINS // FILLS), lambda i: (0, 0, jnp.minimum(i, FILLS - 1))),
            whole((512, 128)),
            *[whole((2, 256, 256)) for _ in range(5)],
        ],
        out_specs=pl.BlockSpec(
            (OWNERS // FILLS, 8, ROWS, 128), lambda i: (jnp.maximum(i - FILLS, 0), 0, 0, 0)
        ),
        out_shape=jax.ShapeDtypeStruct((OWNERS, 8, ROWS, 128), LOW),
        scratch_shapes=[
            pltpu.VMEM((2, 2, 256 * PITCH, 128), F32),
            pltpu.VMEM((8, OWNERS * PITCH, 128), F32),
            pltpu.VMEM((2, 256, 256), F32),
        ],
        name="range_compress",
    )(raw, angles, *tables, turns)


def spread_rows(*pairs):
    def move(n, _):
        for u in range(16 // len(pairs)):
            at = n * (16 // len(pairs)) + u
            for source, xs in pairs:
                for h in range(2):
                    xs[h, pl.ds(at * PITCH, ROWS), :] = source[at, h].astype(F32)
        return 0

    lax.fori_loop(0, OWNERS * len(pairs) // 16, move, 0)


def pulse_rows(xs, p):
    at = pl.ds(p, 128, stride=PITCH)
    return beside(xs[0, at, :], xs[1, at, :])


def picture_kernel(
    re, im, cosine_far, sine_far, full, back, forward_far, backward_far, out,
    xr, xi, ys, vs, ms, cosine, sine, forward, backward, arrived,
):
    step = pl.program_id(0)
    tables = [
        pltpu.make_async_copy(forward_far, forward, arrived.at[0]),
        pltpu.make_async_copy(cosine_far.at[0], cosine.at[0], arrived.at[1]),
        pltpu.make_async_copy(sine_far.at[0], sine.at[0], arrived.at[2]),
        pltpu.make_async_copy(backward_far, backward, arrived.at[3]),
        pltpu.make_async_copy(cosine_far.at[1], cosine.at[1], arrived.at[4]),
        pltpu.make_async_copy(sine_far.at[1], sine.at[1], arrived.at[5]),
    ]

    @pl.when(step == 0)
    def _():
        for table in tables:
            table.start()

    spread_rows((re, xr), (im, xi))

    def outer(p, _):
        x = above(pulse_rows(xr, p), pulse_rows(xi, p)).astype(LOW)
        ys[p] = dot(full[...], x).astype(LOW)
        return 0

    lax.fori_loop(0, 16, outer, 0, unroll=16)

    @pl.when(step == 0)
    def _():
        for table in tables[:4]:
            table.wait()

    @pl.when(step == 1)
    def _():
        for table in tables[4:]:
            table.wait()

    def inner(n, _):
        at = [n * 8 + u for u in range(8)]
        rows = [pl.ds(pl.multiple_of(g * 16, 16), 16) for g in at]
        ahead = [dot(forward[g], ys[:, r, :].reshape(256, 256)) for g, r in zip(at, rows)]
        turned = []
        for g, y in zip(at, ahead):
            y = groups(y)
            c = cosine[step, g].reshape(16, 8, 256)
            s = sine[step, g].reshape(16, 8, 256)
            z = jnp.stack(turned_on(y[:, 0], y[:, 1], c, s), 1)
            turned.append(flat(z).astype(LOW))
        for g, r, z in zip(at, rows, turned):
            vs[:, r, :] = dot(backward[g], z).astype(LOW).reshape(16, 16, 256)
        return 0

    lax.fori_loop(0, 2, inner, 0)

    def last(p, _):
        x = dot(back[...], vs[p])
        x = groups(x)
        a, b = flat(x[:, 0]), flat(x[:, 1])
        m = a * a + b * b
        m = m * lax.rsqrt(jnp.maximum(m, SMALLEST))
        at = pl.ds(p, 128, stride=PITCH)
        ms[0, at, :] = m[:, :128]
        ms[1, at, :] = m[:, 128:]
        return 0

    lax.fori_loop(0, 16, last, 0, unroll=16)

    def gather(n, _):
        for u in range(8):
            at = n * 8 + u
            for h in range(2):
                out[at, h] = ms[h, pl.ds(at * PITCH, ROWS), :].astype(LOW)
        return 0

    lax.fori_loop(0, 16, gather, 0)


def azimuth_picture(received, cosine, sine, full, back, forward, backward):
    return pl.pallas_call(
        picture_kernel,
        grid=(2,),
        in_specs=[
            pl.BlockSpec((OWNERS, 2, ROWS, 128), lambda i: (0, i, 0, 0)),
            pl.BlockSpec((OWNERS, 2, ROWS, 128), lambda i: (0, i + 2, 0, 0)),
            pl.BlockSpec(memory_space=pltpu.HBM),
            pl.BlockSpec(memory_space=pltpu.HBM),
            whole((256, 256)),
            whole((256, 256)),
            pl.BlockSpec(memory_space=pltpu.HBM),
            pl.BlockSpec(memory_space=pltpu.HBM),
        ],
        out_specs=pl.BlockSpec((OWNERS, 2, ROWS, 128), lambda i: (0, i, 0, 0)),
        out_shape=pltpu.HBM((OWNERS, 4, ROWS, 128), LOW),
        scratch_shapes=[
            pltpu.VMEM((2, OWNERS * PITCH, 128), F32),
            pltpu.VMEM((2, OWNERS * PITCH, 128), F32),
            pltpu.VMEM((16, 256, 256), LOW),
            pltpu.VMEM((16, 256, 256), LOW),
            pltpu.VMEM((2, OWNERS * PITCH, 128), F32),
            pltpu.VMEM((2, 16, 128, 256), F32),
            pltpu.VMEM((2, 16, 128, 256), F32),
            pltpu.VMEM((16, 256, 256), LOW),
            pltpu.VMEM((16, 256, 256), LOW),
            pltpu.SemaphoreType.DMA((6,)),
        ],
        name="azimuth_picture",
    )(received, received, cosine, sine, full, back, forward, backward)


def edge_kernel(mag, weights, full, back, forward, backward, out, xs, ys, vs, ms):
    spread_rows((mag, xs))

    def outer(p, _):
        ys[p] = dot(full[:, :128], pulse_rows(xs, p).astype(LOW)).astype(LOW)
        return 0

    lax.fori_loop(0, 16, outer, 0, unroll=4)

    def inner(g, _):
        rows = pl.ds(pl.multiple_of(g * 16, 16), 16)
        y = dot(forward[g], ys[:, rows, :].reshape(256, 256)).reshape(16, 2, 8, 256)
        w = weights[g]
        w = beside(w, w).reshape(16, 8, 256)
        z = jnp.stack([-y[:, 1] * w, y[:, 0] * w], 1).reshape(256, 256).astype(LOW)
        vs[:, rows, :] = dot(backward[g], z).astype(LOW).reshape(16, 16, 256)
        return 0

    lax.fori_loop(0, 16, inner, 0, unroll=2)

    def last(p, _):
        x = dot(back[...], vs[p])
        at = pl.ds(p, 128, stride=PITCH)
        ms[0, at, :] = x[:, :128]
        ms[1, at, :] = x[:, 128:]
        return 0

    lax.fori_loop(0, 16, last, 0, unroll=4)

    def gather(n, _):
        for u in range(8):
            at = n * 8 + u
            rows = pl.ds(pl.multiple_of(at * ROWS, ROWS), ROWS)
            for h in range(2):
                out[rows, h * 128 : h * 128 + 128] = ms[h, pl.ds(at * PITCH, ROWS), :]
        return 0

    lax.fori_loop(0, 16, gather, 0)


def azimuth_edges(mag, weights, full, back, forward, backward):
    return pl.pallas_call(
        edge_kernel,
        grid=(2,),
        in_specs=[
            pl.BlockSpec((OWNERS, 2, ROWS, 128), lambda i: (0, i, 0, 0)),
            whole((16, 128, 128)),
            whole((256, 256)),
            whole((128, 256)),
            whole((16, 256, 256)),
            whole((16, 256, 256)),
        ],
        out_specs=pl.BlockSpec((PULSES, 256), lambda i: (0, i)),
        out_shape=jax.ShapeDtypeStruct((PULSES, WIDTH), F32),
        scratch_shapes=[
            pltpu.VMEM((2, OWNERS * PITCH, 128), F32),
            pltpu.VMEM((16, 256, 256), LOW),
            pltpu.VMEM((16, 256, 256), LOW),
            pltpu.VMEM((2, OWNERS * PITCH, 128), F32),
        ],
        name="azimuth_edges",
    )(mag, weights, full, back, forward, backward)


def concentrate_kernel(mag, weights, first, second, third, last, turns, out, xs, os):
    step = pl.program_id(0)

    @pl.when(step < 2)
    def _():
        def spread(n, _):
            for u in range(4):
                at = n * 4 + u
                for k in range(4):
                    v = mag[at, k].astype(F32)
                    xs[k, pl.ds((step * (OWNERS // 2) + at) * PITCH, ROWS), :] = v
            return 0

        lax.fori_loop(0, OWNERS // 8, spread, 0)

    @pl.when(step == 1)
    def _():
        concentrate_pulses(weights, first, second, third, last, turns, xs, os)

    @pl.when(step >= 2)
    def _():
        def gather(n, _):
            for u in range(4):
                at = n * 4 + u
                rows = pl.ds(((step - 2) * (256 // FILLS) + at) * PITCH, ROWS)
                lanes = pl.ds(pl.multiple_of(at * 256, 256), 256)
                out[:, lanes] = beside(os[0, rows, :], os[1, rows, :])
            return 0

        lax.fori_loop(0, 64 // FILLS, gather, 0)


def concentrate_pulses(weights, first, second, third, last, turns, xs, os):
    top = lax.broadcasted_iota(jnp.int32, (8, 256), 0) == 0

    def one(p):
        at = pl.ds(p, 128, stride=PITCH)
        x = above(beside(xs[0, at, :], xs[1, at, :]), beside(xs[2, at, :], xs[3, at, :]))
        y = groups(dot(first[...], x.astype(LOW)))
        yield
        re, im = flat(y[:, 0]), flat(y[:, 1])
        mirror = jnp.where(top, im[:8], 0.0)
        im = above(jnp.where(top, 0.0, im[:8]), im[8:])
        c, s = groups(turns[0]), groups(turns[1])
        body = sum_and_gap(*turned_back(re, im, flat(c[:, 0]), flat(s[:, 0])))
        tail = sum_and_gap(mirror * c[0, 1], -mirror * s[0, 1])
        rows = [jnp.concatenate([body[e], tail[e], jnp.zeros_like(tail[e])], 0) for e in range(2)]
        zs = yield (rows[0].astype(LOW), rows[1].astype(LOW), second)
        jumped = []
        for e in range(2):
            re, im = halves(zs[e])
            w = weights[:, e * 128 : e * 128 + 128]
            jumped.append(beside(-im * w, re * w).astype(LOW))
        even, odd = yield (jumped[0], jumped[1], third)
        res, ims = [], []
        for h, b in enumerate((even + odd, even - odd)):
            at = slice(h * 128, h * 128 + 128)
            re, im = halves(b)
            c = groups(turns[0])[..., at]
            s = groups(turns[1])[..., at]
            r, i = turned_on(re[:128], im[:128], flat(c[:, 0]), flat(s[:, 0]))
            mirror = re[128:136] * c[0, 1] - im[128:136] * s[0, 1]
            res.append(r)
            ims.append(above(jnp.where(top[:, :128], mirror, i[:8]), i[8:]))
        yield
        e = dot(last[...], above(beside(*res), beside(*ims)).astype(LOW))
        for o in range(2):
            for h in range(2):
                os[h, pl.ds(o * PITCH + p, 128, stride=2 * PITCH), :] = e[
                    o * 128 : o * 128 + 128, h * 128 : h * 128 + 128
                ]

    def some(i, _):
        together([one(4 * i + u) for u in range(4)])
        return 0

    lax.fori_loop(0, ROWS // 4, some, 0)


def range_concentrate(mag, weights, first, second, third, last, turns):
    return pl.pallas_call(
        concentrate_kernel,
        grid=(2 + FILLS,),
        in_specs=[
            pl.BlockSpec((OWNERS // 2, 4, ROWS, 128), lambda i: (jnp.minimum(i, 1), 0, 0, 0)),
            whole((144, 256)),
            whole((256, 256)),
            whole((2, 256, 256)),
            whole((2, 256, 256)),
            whole((256, 256)),
            whole((2, 256, 256)),
        ],
        out_specs=pl.BlockSpec((ROWS, BINS // FILLS), lambda i: (0, jnp.maximum(i - 2, 0))),
        out_shape=jax.ShapeDtypeStruct((ROWS, BINS), F32),
        scratch_shapes=[
            pltpu.VMEM((4, OWNERS * PITCH, 128), F32),
            pltpu.VMEM((2, 256 * PITCH, 128), F32),
        ],
        compiler_params=pltpu.CompilerParams(vmem_limit_bytes=32 << 20),
        name="range_concentrate",
    )(mag, weights, first, second, third, last, turns)


def signed(freqs, length):
    return jnp.where(freqs < length // 2, freqs, freqs - length)


def split_grid(values):
    grid = values.reshape(128, 2, 256)
    return grid.transpose(2, 1, 0).reshape(256, 256)


def azimuth_phase(rates):
    freqs = jnp.arange(PULSES, dtype=jnp.int32).reshape(16, 16, 8).transpose(1, 0, 2)
    s = signed(freqs, PULSES).astype(F32).reshape(1, 16, 128, 1) / PULSES
    angles = (s * s) * rates.reshape(2, 1, 1, 256)
    return jnp.cos(angles), jnp.sin(angles)


def azimuth_weights(factors):
    freqs = jnp.arange(PULSES, dtype=jnp.int32)
    values = jnp.sign(signed(freqs, PULSES)).astype(F32) * factors
    values = values.reshape(16, 16, 8).transpose(1, 0, 2).reshape(16, 128, 1)
    return jnp.broadcast_to(values, (16, 128, 128))


def range_weights(factors):
    freqs = jnp.arange(BINS, dtype=jnp.int32)
    signs = jnp.sign(signed(freqs, BINS)).astype(F32)
    partner = jnp.roll(jnp.flip(factors), 1)
    inside = freqs % 128 != 0
    values = signs * jnp.where(inside, factors + partner, factors)
    return split_grid(values)[:144]


def expand(compact):
    row = lax.broadcasted_iota(jnp.int32, (1, 1, 8, 256), 2)
    lane = lax.broadcasted_iota(jnp.int32, (1, 1, 8, 256), 3)
    kept = jnp.where(lane % 8 == row, compact[:, :, None, :], jnp.zeros((), LOW))
    return kept.reshape(16, 256, 256)


def on_device(raw_pulses, range_phase, azimuth_rate, conc_azimuth, conc_range):
    first, second, third, fourth = range_tables()
    turns = jnp.asarray(range_turns())
    angles = range_phase.reshape(512, 128)
    blocks = range_compress(raw_pulses, angles, (first, second, third, fourth), turns)
    received = lax.all_to_all(blocks, AXES, split_axis=0, concat_axis=0, tiled=True)
    full, back, real_back, forward, backward = azimuth_tables()
    forward, backward, _ = lax.optimization_barrier((forward, backward, conc_azimuth))
    forward, backward = expand(forward), expand(backward)
    cosine, sine = azimuth_phase(azimuth_rate)
    mag = azimuth_picture(received, cosine, sine, full, back, forward, backward)
    shared = lax.all_to_all(mag, AXES, split_axis=0, concat_axis=0, tiled=True)
    edge_azimuth = azimuth_edges(
        mag, azimuth_weights(conc_azimuth), full, real_back, forward, backward
    )
    real_first, real_last = real_range_tables()
    edge_range = range_concentrate(
        shared, range_weights(conc_range), real_first, second, third, real_last, turns
    )
    return (edge_azimuth, edge_range)


def solution(mesh):
    in_specs = (P(None, AXES, None), P(), P(AXES), P(), P())
    out_specs = (P(None, AXES), P(AXES, None))
    return jax.shard_map(
        on_device, mesh=mesh, in_specs=in_specs, out_specs=out_specs, check_vma=False
    )
```

```python
import math

import jax
import jax.numpy as jnp
import numpy as np
from jax import lax
from jax.experimental import pallas as pl
from jax.experimental.pallas import tpu as pltpu
from jax.sharding import PartitionSpec as P

AXES = ("rg", "az")
BINS = 65536
PULSES = 2048
ROWS = 16
PITCH = 18
NARROW = 9
SMALLEST = float(np.finfo(np.float32).tiny)
FILLS = 4
OWNERS = 128
WIDTH = 512
LOW = jnp.bfloat16
F32 = jnp.float32


def roots(exponents, length):
    angles = 2.0 * math.pi / length * (exponents % length)
    return np.cos(angles) + 1j * np.sin(angles)


def left_form(matrix):
    return np.block([[matrix.real, -matrix.imag], [matrix.imag, matrix.real]])


def right_form(matrix):
    return np.block([[matrix.real, matrix.imag], [-matrix.imag, matrix.real]])


def paired(matrix):
    return matrix.reshape(2, 16, 8, -1).transpose(1, 0, 2, 3).reshape(256, -1)


def low(table):
    return np.asarray(table, np.float32).astype(LOW)


def range_tables():
    k = np.arange(128)[:, None]
    j = np.arange(128)[None, :]
    even = roots(2 * j * k, 256) / 16.0
    odd = roots((2 * j + 1) * k, 256) / 16.0
    first = np.stack([paired(left_form(even.conj())), paired(left_form(odd.conj()))])
    second = np.stack([right_form(even.conj()), right_form(odd.conj())])
    third = np.stack([right_form(even.T), right_form(odd.T)])
    fourth = np.stack([left_form(even.T), left_form(odd.T)])
    return tuple(low(t) for t in (first, second, third, fourth))


def range_turns():
    table = paired(roots(np.arange(256)[:, None] * np.arange(256)[None, :], BINS))
    return np.stack([table.real, table.imag]).astype(np.float32)


def real_range_tables():
    k = np.arange(128)[:, None]
    n = np.concatenate([2 * np.arange(128), 2 * np.arange(128) + 1])[None, :]
    base = roots(k * n, 256) / 16.0
    mirror = np.cos(math.pi * n) / 16.0
    first = np.concatenate([base.real, mirror, -base.imag[1:]], 0)
    last = np.concatenate([base.real.T, mirror.T, -base.imag[1:].T], 1)
    return low(paired(first)), low(last)


def azimuth_tables():
    s = np.arange(128)
    outer = roots(-s[:, None] * s[None, :], 128) / math.sqrt(128.0)
    full = paired(left_form(outer))
    group = np.arange(16)[:, None, None, None]
    eight = np.arange(8)[None, None, None, :]
    fb = np.arange(16)[None, :, None, None]
    p = np.arange(16)[None, None, :, None]
    inner = roots(-p * (8 * group + eight + 128 * fb), PULSES) / 4.0
    pair = np.stack([np.stack([inner.real, -inner.imag], 3), np.stack([inner.imag, inner.real], 3)], 2)
    forward = pair.reshape(16, 32, 256)
    backward = pair.transpose(0, 3, 4, 1, 2, 5).reshape(16, 32, 256)
    return low(full), low(paired(full.T)), low(full.T[:128]), low(forward), low(backward)


def dot(a, b):
    return jnp.dot(a, b, preferred_element_type=F32)


def beside(a, b):
    return jnp.concatenate([a, b], 1)


def above(a, b):
    return jnp.concatenate([a, b], 0)


def whole(shape):
    return pl.BlockSpec(shape, lambda i: (0,) * len(shape), pipeline_mode=pl.Buffered(1))


def together(jobs):
    asked = [next(job) for job in jobs]
    while asked:
        sent = [None] * len(jobs)
        if asked[0] is not None:
            rows = asked[0][0].shape[0]
            results = []
            for e in range(2):
                lhs = jnp.concatenate([ask[e] for ask in asked], 0)
                results.append(dot(lhs, asked[0][2][e]))
            sent = [[r[n * rows : n * rows + rows] for r in results] for n in range(len(jobs))]
        nexts = []
        for job, value in zip(jobs, sent):
            try:
                nexts.append(job.send(value))
            except StopIteration:
                pass
        asked = nexts


def groups(value):
    return value.reshape(-1, 2, 8, value.shape[-1])


def halves(value):
    return value[..., :128], value[..., 128:]


def flat(value):
    return value.reshape(-1, value.shape[-1])


def turned_back(re, im, c, s):
    return re * c + im * s, im * c - re * s


def turned_on(re, im, c, s):
    return re * c - im * s, re * s + im * c


def sum_and_gap(re, im):
    (r0, r1), (i0, i1) = halves(re), halves(im)
    join = lambda a, b: jnp.concatenate([a, b], -1)
    return join(r0 + r1, i0 + i1), join(r0 - r1, i0 - i1)


def sine_cosine(x):
    t = 0.5 * x
    u = t * t
    s = 1.0 / 39916800.0
    for k in (362880.0, -5040.0, 120.0, -6.0, 1.0):
        s = 1.0 / k + u * s if k != 362880.0 else 1.0 / k - u * s
    s = s * t
    c = 1.0 / 479001600.0
    for k in (-3628800.0, 40320.0, -720.0, 24.0, -2.0, 1.0):
        c = 1.0 / k + u * c
    return 2.0 * s * c, 1.0 - 2.0 * s * s


def compress_kernel(
    raw_far, angles_far, first_far, second_far, third_far, fourth_far, turns_far, out_far,
    raw, angles, first, second, third, fourth, turns, xs, os, phase, packed, arrived, left,
):
    here = [
        (angles_far, angles),
        (raw_far.at[:, pl.ds(0, 8), :], raw.at[0]),
        (turns_far, turns),
        (first_far, first),
        (second_far, second),
        (third_far, third),
        (fourth_far, fourth),
    ]
    here.append((raw_far.at[:, pl.ds(8, 8), :], raw.at[1]))
    here = [pltpu.make_async_copy(a, b, arrived.at[n]) for n, (a, b) in enumerate(here)]
    for copy in here:
        copy.start()

    def sending(half, part):
        some = pl.ds(part * (OWNERS // 2), OWNERS // 2)
        return pltpu.make_async_copy(
            packed.at[half, some], out_far.at[some, half], left.at[2 * half + part]
        )

    def spread(half, n):
        lane, row = pl.multiple_of(n * 4096, 4096), n * (16 * NARROW)
        for c in range(2):
            v = raw[half, c, :, pl.ds(lane, 4096)]
            for u in range(16):
                for h in range(2):
                    at = (2 * u + h) * 128
                    xs[half, c, h, pl.ds(row + u * NARROW, 8), :] = v[:, at : at + 128].astype(F32)

    def gather(half, n):
        base, row = n * 8, n * (8 * PITCH)
        for u in range(8):
            for k in range(4):
                v = os[half, k, pl.ds(row + u * PITCH, ROWS), :]
                packed[half, base + u, k] = v.astype(LOW)

    def one(half, p):
        def load(odd):
            def wide(c):
                at = pl.ds(odd * NARROW + p, 128, stride=2 * NARROW)
                return beside(xs[half, c, 0, at, :], xs[half, c, 1, at, :])

            return above(wide(0), wide(1)).astype(LOW)

        even = groups(dot(first[0], load(0)))
        odd = groups(dot(first[1], load(1)))
        yield
        c, s = groups(turns[0]), groups(turns[1])
        parts = []
        for h, v in enumerate((even + odd, even - odd)):
            parts.append(sum_and_gap(*turned_back(v[:, 0], v[:, 1], c[:, h], s[:, h])))
        zs = [flat(jnp.stack([parts[0][e], parts[1][e]], 1)).astype(LOW) for e in range(2)]
        zs = yield (zs[0], zs[1], second)
        turned = []
        for e in range(2):
            re, im = halves(zs[e])
            at = slice(e * 128, e * 128 + 128)
            turned.append(beside(*turned_on(re, im, phase[0, :, at], phase[1, :, at])).astype(LOW))
        even, odd = yield (turned[0], turned[1], third)
        even, odd = groups(even), groups(odd)
        sums, gaps = [], []
        for h, b in enumerate((even + odd, even - odd)):
            at = slice(h * 128, h * 128 + 128)
            re, im = halves(b)
            re, im = turned_on(re, im, groups(turns[0])[..., at], groups(turns[1])[..., at])
            sums.append((flat(re[:, 0] + re[:, 1]), flat(im[:, 0] + im[:, 1])))
            gaps.append((flat(re[:, 0] - re[:, 1]), flat(im[:, 0] - im[:, 1])))
        sums, gaps = (
            above(beside(v[0][0], v[1][0]), beside(v[0][1], v[1][1])).astype(LOW)
            for v in (sums, gaps)
        )
        yield
        for o, c in enumerate((dot(fourth[0], sums), dot(fourth[1], gaps))):
            for part in range(2):
                for h in range(2):
                    os[half, o * 2 + h, pl.ds(part * 8 + p, 128, stride=PITCH), :] = c[
                        part * 128 : part * 128 + 128, h * 128 : h * 128 + 128
                    ]

    here[0].wait()
    for e in range(2):
        for h in range(2):
            part = angles[pl.ds(2 * e + h, 128, stride=4), :]
            sine, cosine = sine_cosine(part.T)
            for t in range(16):
                rows = slice(t * 16 + h * 8, t * 16 + h * 8 + 8)
                phase[0, rows, e * 128 : e * 128 + 128] = cosine[t * 8 : t * 8 + 8]
                phase[1, rows, e * 128 : e * 128 + 128] = sine[t * 8 : t * 8 + 8]

    def one_half(half, _):
        @pl.when(half == 0)
        def _():
            here[1].wait()

        @pl.when(half == 1)
        def _():
            here[7].wait()

        def spread_some(n, _):
            spread(half, n)
            return 0

        lax.fori_loop(0, 16, spread_some, 0)

        @pl.when(half == 0)
        def _():
            for copy in here[2:7]:
                copy.wait()

        def some(i, _):
            together([one(half, 4 * i + u) for u in range(4)])
            return 0

        lax.fori_loop(0, 2, some, 0)

        def gather_part(part, _):
            def gather_some(n, _):
                gather(half, part * 8 + n)
                return 0

            lax.fori_loop(0, 8, gather_some, 0)
            sending(half, part).start()
            return 0

        lax.fori_loop(0, 2, gather_part, 0)
        return 0

    lax.fori_loop(0, 2, one_half, 0)
    for half in range(2):
        for part in range(2):
            sending(half, part).wait()


def range_compress(raw, angles, tables, turns):
    far = pl.BlockSpec(memory_space=pltpu.HBM)
    return pl.pallas_call(
        compress_kernel,
        in_specs=[far] * 7,
        out_specs=far,
        out_shape=pltpu.HBM((OWNERS, 2, 4, ROWS, 128), LOW),
        scratch_shapes=[
            pltpu.VMEM((2, 2, 8, BINS), LOW),
            pltpu.VMEM((512, 128), F32),
            *[pltpu.VMEM((2, 256, 256), LOW) for _ in range(4)],
            pltpu.VMEM((2, 256, 256), F32),
            pltpu.VMEM((2, 2, 2, 256 * NARROW, 128), F32),
            pltpu.VMEM((2, 4, OWNERS * PITCH, 128), F32),
            pltpu.VMEM((2, 256, 256), F32),
            pltpu.VMEM((2, OWNERS, 4, ROWS, 128), LOW),
            pltpu.SemaphoreType.DMA((8,)),
            pltpu.SemaphoreType.DMA((4,)),
        ],
        name="range_compress",
    )(raw, angles, *tables, turns)


def spread_rows(*pairs):
    def move(n, _):
        for u in range(16 // len(pairs)):
            at = n * (16 // len(pairs)) + u
            for source, xs in pairs:
                for h in range(2):
                    xs[h, pl.ds(at * PITCH, ROWS), :] = source[at, h].astype(F32)
        return 0

    lax.fori_loop(0, OWNERS * len(pairs) // 16, move, 0)


def pulse_rows(xs, p):
    at = pl.ds(p, 128, stride=PITCH)
    return beside(xs[0, at, :], xs[1, at, :])


def picture_kernel(
    received_far, cosine_far, sine_far, full, back, forward_far, backward_far, out,
    xr, xi, ys, vs, ms, cosine, sine, forward, backward, blocks, arrived,
):
    step = pl.program_id(0)
    here = []
    for c in range(4):
        some = pl.ds(c * 32, 32)
        here.append((received_far.at[some, :, pl.ds(0, 2)], blocks.at[0, some]))
    for h in range(2):
        some = pl.ds(h * 8, 8)
        here.append((forward_far.at[some], forward.at[some]))
        here.append((cosine_far.at[0, some], cosine.at[0, some]))
        here.append((sine_far.at[0, some], sine.at[0, some]))
        here.append((backward_far.at[some], backward.at[some]))
    here.append((received_far.at[:, :, pl.ds(2, 2)], blocks.at[1]))
    here.append((cosine_far.at[1], cosine.at[1]))
    here.append((sine_far.at[1], sine.at[1]))
    here = [pltpu.make_async_copy(a, b, arrived.at[n]) for n, (a, b) in enumerate(here)]

    def await_when(condition, copies):
        @pl.when(condition)
        def _():
            for copy in copies:
                copy.wait()

    @pl.when(step == 0)
    def _():
        for copy in here:
            copy.start()

    await_when(step == 1, here[12:13])
    for c in range(4):
        await_when(step == 0, here[c : c + 1])

        def spread(n, _):
            base = c * 32 + n * 8
            row = base * PITCH
            for u in range(8):
                for part in range(2):
                    rows = pl.ds(row + u * PITCH + part * 8, 8)
                    for h in range(2):
                        v = blocks[step, base + u, part, h].astype(F32)
                        xr[h, rows, :] = v[:8]
                        xi[h, rows, :] = v[8:]
            return 0

        lax.fori_loop(0, 4, spread, 0)

    def outer(p, _):
        x = above(pulse_rows(xr, p), pulse_rows(xi, p)).astype(LOW)
        ys[p] = dot(full[...], x).astype(LOW)
        return 0

    lax.fori_loop(0, 16, outer, 0, unroll=16)

    await_when(step == 1, here[13:15])

    def inner(n, _):
        await_when(jnp.logical_and(step == 0, n == 0), here[4:8])
        await_when(jnp.logical_and(step == 0, n == 1), here[8:12])
        at = [n * 8 + u for u in range(8)]
        rows = [pl.ds(pl.multiple_of(g * 16, 16), 16) for g in at]
        ahead = [dot(forward[g], ys[:, r, :].reshape(256, 256)) for g, r in zip(at, rows)]
        turned = []
        for g, y in zip(at, ahead):
            y = groups(y)
            c = cosine[step, g].reshape(16, 8, 256)
            s = sine[step, g].reshape(16, 8, 256)
            z = jnp.stack(turned_on(y[:, 0], y[:, 1], c, s), 1)
            turned.append(flat(z).astype(LOW))
        for g, r, z in zip(at, rows, turned):
            vs[:, r, :] = dot(backward[g], z).astype(LOW).reshape(16, 16, 256)
        return 0

    lax.fori_loop(0, 2, inner, 0)

    def last(p, _):
        x = dot(back[...], vs[p])
        x = groups(x)
        a, b = flat(x[:, 0]), flat(x[:, 1])
        m = a * a + b * b
        m = m * lax.rsqrt(jnp.maximum(m, SMALLEST))
        at = pl.ds(p, 128, stride=PITCH)
        ms[0, at, :] = m[:, :128]
        ms[1, at, :] = m[:, 128:]
        return 0

    lax.fori_loop(0, 16, last, 0, unroll=16)

    def gather(n, _):
        for u in range(8):
            at = n * 8 + u
            for h in range(2):
                out[at, h] = ms[h, pl.ds(at * PITCH, ROWS), :].astype(LOW)
        return 0

    lax.fori_loop(0, 16, gather, 0)


def azimuth_picture(received, cosine, sine, full, back, forward, backward):
    return pl.pallas_call(
        picture_kernel,
        grid=(2,),
        in_specs=[
            pl.BlockSpec(memory_space=pltpu.HBM),
            pl.BlockSpec(memory_space=pltpu.HBM),
            pl.BlockSpec(memory_space=pltpu.HBM),
            whole((256, 256)),
            whole((256, 256)),
            pl.BlockSpec(memory_space=pltpu.HBM),
            pl.BlockSpec(memory_space=pltpu.HBM),
        ],
        out_specs=pl.BlockSpec((OWNERS, 2, ROWS, 128), lambda i: (0, i, 0, 0)),
        out_shape=pltpu.HBM((OWNERS, 4, ROWS, 128), LOW),
        scratch_shapes=[
            pltpu.VMEM((2, OWNERS * PITCH, 128), F32),
            pltpu.VMEM((2, OWNERS * PITCH, 128), F32),
            pltpu.VMEM((16, 256, 256), LOW),
            pltpu.VMEM((16, 256, 256), LOW),
            pltpu.VMEM((2, OWNERS * PITCH, 128), F32),
            pltpu.VMEM((2, 16, 128, 256), F32),
            pltpu.VMEM((2, 16, 128, 256), F32),
            pltpu.VMEM((16, 256, 256), LOW),
            pltpu.VMEM((16, 256, 256), LOW),
            pltpu.VMEM((2, OWNERS, 2, 2, ROWS, 128), LOW),
            pltpu.SemaphoreType.DMA((15,)),
        ],
        name="azimuth_picture",
    )(received, cosine, sine, full, back, forward, backward)


def edge_kernel(mag, weights, full, back, forward, backward, out, xs, ys, vs, ms):
    spread_rows((mag, xs))

    def outer(p, _):
        ys[p] = dot(full[:, :128], pulse_rows(xs, p).astype(LOW)).astype(LOW)
        return 0

    lax.fori_loop(0, 16, outer, 0, unroll=4)

    def inner(g, _):
        rows = pl.ds(pl.multiple_of(g * 16, 16), 16)
        y = dot(forward[g], ys[:, rows, :].reshape(256, 256)).reshape(16, 2, 8, 256)
        w = weights[g]
        w = beside(w, w).reshape(16, 8, 256)
        z = jnp.stack([-y[:, 1] * w, y[:, 0] * w], 1).reshape(256, 256).astype(LOW)
        vs[:, rows, :] = dot(backward[g], z).astype(LOW).reshape(16, 16, 256)
        return 0

    lax.fori_loop(0, 16, inner, 0, unroll=2)

    def last(p, _):
        x = dot(back[...], vs[p])
        at = pl.ds(p, 128, stride=PITCH)
        ms[0, at, :] = x[:, :128]
        ms[1, at, :] = x[:, 128:]
        return 0

    lax.fori_loop(0, 16, last, 0, unroll=4)

    def gather(n, _):
        for u in range(8):
            at = n * 8 + u
            rows = pl.ds(pl.multiple_of(at * ROWS, ROWS), ROWS)
            for h in range(2):
                out[rows, h * 128 : h * 128 + 128] = ms[h, pl.ds(at * PITCH, ROWS), :]
        return 0

    lax.fori_loop(0, 16, gather, 0)


def azimuth_edges(mag, weights, full, back, forward, backward):
    return pl.pallas_call(
        edge_kernel,
        grid=(2,),
        in_specs=[
            pl.BlockSpec((OWNERS, 2, ROWS, 128), lambda i: (0, i, 0, 0)),
            whole((16, 128, 128)),
            whole((256, 256)),
            whole((128, 256)),
            whole((16, 256, 256)),
            whole((16, 256, 256)),
        ],
        out_specs=pl.BlockSpec((PULSES, 256), lambda i: (0, i)),
        out_shape=jax.ShapeDtypeStruct((PULSES, WIDTH), F32),
        scratch_shapes=[
            pltpu.VMEM((2, OWNERS * PITCH, 128), F32),
            pltpu.VMEM((16, 256, 256), LOW),
            pltpu.VMEM((16, 256, 256), LOW),
            pltpu.VMEM((2, OWNERS * PITCH, 128), F32),
        ],
        name="azimuth_edges",
    )(mag, weights, full, back, forward, backward)


def concentrate_kernel(mag, weights, first, second, third, last, turns, out, xs, os):
    step = pl.program_id(0)

    @pl.when(step < 2)
    def _():
        def spread(n, _):
            row = (step * (OWNERS // 2) + n * 8) * PITCH
            for u in range(8):
                for k in range(4):
                    xs[k, pl.ds(row + u * PITCH, ROWS), :] = mag[n * 8 + u, k].astype(F32)
            return 0

        lax.fori_loop(0, OWNERS // 16, spread, 0)

    @pl.when(step == 1)
    def _():
        concentrate_pulses(weights, first, second, third, last, turns, xs, os)

    @pl.when(step >= 2)
    def _():
        def gather(n, _):
            row = ((step - 2) * (256 // FILLS) + n * 16) * PITCH
            lane = pl.multiple_of(n * 4096, 4096)
            values = []
            for u in range(16):
                values += [os[h, pl.ds(row + u * PITCH, ROWS), :] for h in range(2)]
            out[:, pl.ds(lane, 4096)] = jnp.concatenate(values, 1)
            return 0

        lax.fori_loop(0, 16 // FILLS, gather, 0)


def concentrate_pulses(weights, first, second, third, last, turns, xs, os):
    top = lax.broadcasted_iota(jnp.int32, (8, 256), 0) == 0

    def one(p):
        at = pl.ds(p, 128, stride=PITCH)
        x = above(beside(xs[0, at, :], xs[1, at, :]), beside(xs[2, at, :], xs[3, at, :]))
        y = groups(dot(first[...], x.astype(LOW)))
        yield
        re, im = flat(y[:, 0]), flat(y[:, 1])
        mirror = jnp.where(top, im[:8], 0.0)
        im = above(jnp.where(top, 0.0, im[:8]), im[8:])
        c, s = groups(turns[0]), groups(turns[1])
        body = sum_and_gap(*turned_back(re, im, flat(c[:, 0]), flat(s[:, 0])))
        tail = sum_and_gap(mirror * c[0, 1], -mirror * s[0, 1])
        rows = [jnp.concatenate([body[e], tail[e], jnp.zeros_like(tail[e])], 0) for e in range(2)]
        zs = yield (rows[0].astype(LOW), rows[1].astype(LOW), second)
        jumped = []
        for e in range(2):
            re, im = halves(zs[e])
            w = weights[:, e * 128 : e * 128 + 128]
            jumped.append(beside(-im * w, re * w).astype(LOW))
        even, odd = yield (jumped[0], jumped[1], third)
        res, ims = [], []
        for h, b in enumerate((even + odd, even - odd)):
            at = slice(h * 128, h * 128 + 128)
            re, im = halves(b)
            c = groups(turns[0])[..., at]
            s = groups(turns[1])[..., at]
            r, i = turned_on(re[:128], im[:128], flat(c[:, 0]), flat(s[:, 0]))
            mirror = re[128:136] * c[0, 1] - im[128:136] * s[0, 1]
            res.append(r)
            ims.append(above(jnp.where(top[:, :128], mirror, i[:8]), i[8:]))
        yield
        e = dot(last[...], above(beside(*res), beside(*ims)).astype(LOW))
        for o in range(2):
            for h in range(2):
                os[h, pl.ds(o * PITCH + p, 128, stride=2 * PITCH), :] = e[
                    o * 128 : o * 128 + 128, h * 128 : h * 128 + 128
                ]

    def some(i, _):
        together([one(4 * i + u) for u in range(4)])
        return 0

    lax.fori_loop(0, ROWS // 4, some, 0)


def range_concentrate(mag, weights, first, second, third, last, turns):
    return pl.pallas_call(
        concentrate_kernel,
        grid=(2 + FILLS,),
        in_specs=[
            pl.BlockSpec((OWNERS // 2, 4, ROWS, 128), lambda i: (jnp.minimum(i, 1), 0, 0, 0)),
            whole((144, 256)),
            whole((256, 256)),
            whole((2, 256, 256)),
            whole((2, 256, 256)),
            whole((256, 256)),
            whole((2, 256, 256)),
        ],
        out_specs=pl.BlockSpec((ROWS, BINS // FILLS), lambda i: (0, jnp.maximum(i - 2, 0))),
        out_shape=jax.ShapeDtypeStruct((ROWS, BINS), F32),
        scratch_shapes=[
            pltpu.VMEM((4, OWNERS * PITCH, 128), F32),
            pltpu.VMEM((2, 256 * PITCH, 128), F32),
        ],
        compiler_params=pltpu.CompilerParams(vmem_limit_bytes=32 << 20),
        name="range_concentrate",
    )(mag, weights, first, second, third, last, turns)


def signed(freqs, length):
    return jnp.where(freqs < length // 2, freqs, freqs - length)


def split_grid(values):
    grid = values.reshape(128, 2, 256)
    return grid.transpose(2, 1, 0).reshape(256, 256)


def azimuth_phase(rates):
    freqs = jnp.arange(PULSES, dtype=jnp.int32).reshape(16, 16, 8).transpose(1, 0, 2)
    s = signed(freqs, PULSES).astype(F32).reshape(1, 16, 128, 1) / PULSES
    angles = (s * s) * rates.reshape(2, 1, 1, 256)
    return jnp.cos(angles), jnp.sin(angles)


def azimuth_weights(factors):
    freqs = jnp.arange(PULSES, dtype=jnp.int32)
    values = jnp.sign(signed(freqs, PULSES)).astype(F32) * factors
    values = values.reshape(16, 16, 8).transpose(1, 0, 2).reshape(16, 128, 1)
    return jnp.broadcast_to(values, (16, 128, 128))


def range_weights(factors):
    freqs = jnp.arange(BINS, dtype=jnp.int32)
    signs = jnp.sign(signed(freqs, BINS)).astype(F32)
    partner = jnp.roll(jnp.flip(factors), 1)
    inside = freqs % 128 != 0
    values = signs * jnp.where(inside, factors + partner, factors)
    return split_grid(values)[:144]


def expand(compact):
    row = lax.broadcasted_iota(jnp.int32, (1, 1, 8, 256), 2)
    lane = lax.broadcasted_iota(jnp.int32, (1, 1, 8, 256), 3)
    kept = jnp.where(lane % 8 == row, compact[:, :, None, :], jnp.zeros((), LOW))
    return kept.reshape(16, 256, 256)


def on_device(raw_pulses, range_phase, azimuth_rate, conc_azimuth, conc_range):
    first, second, third, fourth = range_tables()
    turns = jnp.asarray(range_turns())
    angles = range_phase.reshape(512, 128)
    blocks = range_compress(raw_pulses, angles, (first, second, third, fourth), turns)
    received = lax.all_to_all(blocks, AXES, split_axis=0, concat_axis=0, tiled=True)
    full, back, real_back, forward, backward = azimuth_tables()
    forward, backward, _ = lax.optimization_barrier((forward, backward, conc_azimuth))
    forward, backward = expand(forward), expand(backward)
    cosine, sine = azimuth_phase(azimuth_rate)
    mag = azimuth_picture(received, cosine, sine, full, back, forward, backward)
    shared = lax.all_to_all(mag, AXES, split_axis=0, concat_axis=0, tiled=True)
    edge_azimuth = azimuth_edges(
        mag, azimuth_weights(conc_azimuth), full, real_back, forward, backward
    )
    real_first, real_last = real_range_tables()
    edge_range = range_concentrate(
        shared, range_weights(conc_range), real_first, second, third, real_last, turns
    )
    return (edge_azimuth, edge_range)


def solution(mesh):
    in_specs = (P(None, AXES, None), P(), P(AXES), P(), P())
    out_specs = (P(None, AXES), P(AXES, None))
    return jax.shard_map(
        on_device, mesh=mesh, in_specs=in_specs, out_specs=out_specs, check_vma=False
    )
```
